128 devices in a mesh: users: 32 (over z, x, core), items: 4 (over y).
Axes of the slice: x: 4, y: 4, z: 4, core: 2. Of those that a mesh axis runs over, the one named last changes fastest.
Arguments:
- user_factors: bfloat16 [65536, 256], P('users'), may hold values from -1.5 to 1.5
- item_factors: bfloat16 [4, 4096, 256], P('items', 'users'), may hold values from -1.5 to 1.5
- confidence: bfloat16 [32, 4, 256, 128, 128], P('users', 'items'), may hold values from 0.099609375 to 10
- tile_counts: int32 [32, 4, 256], P('users', 'items'), may hold values from 1 to 4095
- tile_user: int32 [32, 4, 256], P('users', 'items'), may hold values from 0 to 15
- tile_item: int32 [32, 4, 256], P('users', 'items'), may hold values from 0 to 31
- block_slot: int32 [4, 32], P('items'), may hold values from 0 to 31, each once within a row
- live_tiles: int32 [32, 4], P('users', 'items'), may hold values from 64 to 256, as said below
Outputs:
- user_grad: float32 [65536, 256], P('users')
- item_grad: float32 [4, 4096, 256], P('items', 'users')
The draws below stay inside these ranges and needn't reach their ends.
Inputs may be any that keep to these rules, and one draw needn't show every extreme that they name: Tile slots at positions from live_tiles on are ignored; some user shard and group uses all 256 slots.
All inputs are finite; a program needn't handle non-finite values.
Results may differ from the reference program's by a relative error of at most 0.0012.
Values may be sent and summed in bfloat16 or wider, within the bound.
No kernel may reach another device: no remote copies, remote signals or barrier semaphores. Data moves between devices by JAX's collectives and lax.ppermute only.
A program may use at most 128 MiB of HBM per device.

```python
import math
import jax
import jax.numpy as jnp
from jax import lax

K = 256
TILE = 128
UB_DEV = 16
TILES_DEV = 256
NB_G = 32
NI_G = 4096
NU = 65536
N_USERS = 32
N_ITEMS = 4


def draw_live_tiles(key, part):
    key_one, key_two = jax.random.split(key)
    lowest = max(1, TILES_DEV // 4)
    values = jax.random.randint(key_one, (N_USERS * N_ITEMS,), lowest, TILES_DEV + 1, dtype=jnp.int32)
    chosen = jax.random.randint(key_two, (), 0, N_USERS * N_ITEMS, dtype=jnp.int32)
    values = jnp.where(jnp.arange(N_USERS * N_ITEMS, dtype=jnp.int32) == chosen, TILES_DEV, values)
    return values.reshape(N_USERS, N_ITEMS).astype(jnp.int32)


def with_ends(entries, rng, least, high):
    dims = entries.shape
    place = [jax.random.randint(jax.random.fold_in(rng, axis), (), 0, dims[axis]) for axis in range(len(dims))]
    entries = entries.at[tuple(place)].set(least)
    longest = dims.index(max(dims))
    place[longest] = (place[longest] + 1) % dims[longest]
    return entries.at[tuple(place)].set(high)


def block_scale(own_key, shape, shards, low, top_value):
    level = 1.0
    for axis_at, shards_of in shards:
        draws = jax.random.uniform(jax.random.fold_in(jax.random.fold_in(own_key, 6), axis_at), (shards_of,), jnp.float32, low / len(shards), top_value / len(shards))
        level = level * jnp.repeat(jnp.exp(draws), shape[axis_at] // shards_of).reshape((-1,) + (1,) * (len(shape) - 1 - axis_at))
    return level


def bell_draw(rng, dims, spread, most, cuts=(), kind=jnp.bfloat16):
    values = jax.random.normal(rng, dims, jnp.float32) * spread
    if len(cuts) > 0:
        values = block_scale(rng, dims, cuts, -0.22, 0.18) * values
    return jnp.clip(values, min=-most, max=most).astype(kind)


def setup_inputs(seed: int = 0) -> dict:
    seeds = jax.random.split(jax.random.key(seed), 9)
    return {
        "user_factors": bell_draw(seeds[0], (NU, K), 0.25, 1.5, ((0, 32),)),
        "item_factors": bell_draw(seeds[1], (N_ITEMS, NI_G, K), 0.25, 1.5, ((0, 4), (1, 32))),
        "confidence": jnp.clip(jnp.exp(math.log(10.0) - 4.609084 * jax.random.uniform(seeds[2], (N_USERS, N_ITEMS, TILES_DEV, TILE, TILE), jnp.float32) ** block_scale(seeds[2], (N_USERS, N_ITEMS, TILES_DEV, TILE, TILE), ((0, 32), (1, 4)), -0.2, 0.2)), 0.099609375, 10.0).astype(jnp.bfloat16),
        "tile_counts": with_ends(jax.random.randint(seeds[3], (N_USERS, N_ITEMS, TILES_DEV), 1, 4096), jax.random.fold_in(seeds[3], 1), 1, 4095).astype(jnp.int32),
        "tile_user": with_ends(jax.random.randint(seeds[4], (N_USERS, N_ITEMS, TILES_DEV), 0, UB_DEV), jax.random.fold_in(seeds[4], 1), 0, UB_DEV - 1).astype(jnp.int32),
        "tile_item": with_ends(jax.random.randint(seeds[5], (N_USERS, N_ITEMS, TILES_DEV), 0, NB_G), jax.random.fold_in(seeds[5], 1), 0, NB_G - 1).astype(jnp.int32),
        "block_slot": jax.vmap(lambda own: jax.random.permutation(own, NB_G))(jax.random.split(seeds[6], N_ITEMS)).reshape((N_ITEMS, NB_G)).astype(jnp.int32),
        "live_tiles": draw_live_tiles(jax.random.fold_in(seeds[8], 71), 0),
    }


grad_scale = 0.005
gram_weight = 0.5


def reference(user_factors, item_factors, confidence, tile_counts, tile_user, tile_item, block_slot, live_tiles):
    tile_total = N_USERS * N_ITEMS * TILES_DEV
    step_tiles = math.gcd(TILES_DEV, 32)
    block_total = tile_total // step_tiles
    user_blocks = user_factors.reshape(N_USERS * UB_DEV, TILE, K)
    item_blocks = item_factors.reshape(N_ITEMS * NB_G, TILE, K)
    shard_of = jnp.arange(N_USERS, dtype=jnp.int32)[:, None, None]
    group_of = jnp.arange(N_ITEMS, dtype=jnp.int32)[None, :, None]
    position = jnp.arange(TILES_DEV, dtype=jnp.int32)[None, None, :]
    user_index = (shard_of * UB_DEV + tile_user).astype(jnp.int32).reshape(block_total, step_tiles)
    slot_index = (group_of * NB_G + block_slot[group_of, tile_item]).astype(jnp.int32).reshape(block_total, step_tiles)
    live_mask = (position < live_tiles[:, :, None]).astype(jnp.float32)
    tile_scale = (jnp.log1p(tile_counts.astype(jnp.float32)) * live_mask).reshape(block_total, step_tiles)
    conf_all = confidence.reshape(block_total, step_tiles, TILE, TILE)

    def visit_block(state_pair, pieces):
        user_acc, item_acc = state_pair
        conf_block, user_pick, slot_pick, scale_pick = pieces
        user_tiles = user_blocks[user_pick].astype(jnp.float32)
        item_tiles = item_blocks[slot_pick].astype(jnp.float32)
        scores = jnp.einsum("tak,tbk->tab", user_tiles, item_tiles)
        weighted = (conf_block.astype(jnp.float32) * scale_pick[:, None, None] * (scores - 1.0)).astype(jnp.bfloat16)
        weighted = weighted.astype(jnp.float32)
        user_terms = jnp.einsum("tab,tbk->tak", weighted, item_tiles)
        item_terms = jnp.einsum("tab,tak->tbk", weighted, user_tiles)
        return (user_acc.at[user_pick].add(user_terms), item_acc.at[slot_pick].add(item_terms)), None

    start_pair = (jnp.zeros((N_USERS * UB_DEV, TILE, K), jnp.float32), jnp.zeros((N_ITEMS * NB_G, TILE, K), jnp.float32))
    (user_acc, item_acc), _ = lax.scan(visit_block, start_pair, (conf_all, user_index, slot_index, tile_scale))
    flat_items = item_factors.reshape(N_ITEMS * NI_G, K)
    item_gram = jnp.dot(flat_items.T, flat_items, preferred_element_type=jnp.float32)
    user_gram = jnp.dot(user_factors.T, user_factors, preferred_element_type=jnp.float32)
    user_side = jnp.dot(user_factors.astype(jnp.float32), item_gram, precision=lax.Precision.HIGHEST)
    item_side = jnp.dot(flat_items.astype(jnp.float32), user_gram, precision=lax.Precision.HIGHEST)
    user_grad = grad_scale * (user_acc.reshape(NU, K) + gram_weight * user_side)
    item_grad = grad_scale * (item_acc.reshape(N_ITEMS * NI_G, K) + gram_weight * item_side)
    return user_grad, item_grad.reshape(N_ITEMS, NI_G, K)
```

```python
import jax
import jax.numpy as jnp
from jax import lax
from jax.experimental import pallas as pl
from jax.experimental.pallas import tpu as pltpu
from jax.sharding import PartitionSpec as P

GRAD_SCALE = 0.005
GRAM_WEIGHT = 0.5
SLOTS = 8


def dot(a, b, ca, cb):
    return lax.dot_general(a, b, (((ca,), (cb,)), ((), ())), preferred_element_type=jnp.float32)


def plan_kernel(user_ref, item_ref, slot_ref, live_ref, scale_ref, head_ref, pair_ref, tile_ref, panel_ref, factor_ref, place_ref):
    user_total = place_ref.shape[0]
    pair_total = pair_ref.shape[0]
    live = live_ref[0]

    def clear_user(u, carry):
        place_ref[u] = 0
        return carry

    lax.fori_loop(0, user_total, clear_user, 0)

    def clear_pair(p, carry):
        tile_ref[p] = 0
        panel_ref[p] = 0
        factor_ref[p] = 0.0
        return carry

    lax.fori_loop(0, 2 * pair_total, clear_pair, 0)

    def count(t, carry):
        u = user_ref[t]
        place_ref[u] = place_ref[u] + 1
        return carry

    lax.fori_loop(0, live, count, 0)

    def start(u, first):
        pairs = (place_ref[u] + 1) // 2
        place_ref[u] = 2 * first

        def name(p, carry):
            pair_ref[p] = u
            return carry

        lax.fori_loop(first, first + pairs, name, 0)
        return first + pairs

    head_ref[0] = lax.fori_loop(0, user_total, start, 0)

    def put(t, carry):
        u = user_ref[t]
        spot = place_ref[u]
        place_ref[u] = spot + 1
        tile_ref[spot] = t
        panel_ref[spot] = slot_ref[item_ref[t]]
        factor_ref[spot] = scale_ref[t]
        return carry

    lax.fori_loop(0, live, put, 0)


def split(x):
    high = x.astype(jnp.bfloat16)
    return high, (x - high.astype(jnp.float32)).astype(jnp.bfloat16)


def tile_kernel(head_ref, pair_ref, tile_ref, panel_ref, factor_ref, users_ref, items_ref, conf_ref, user_out, item_out, conf_buf, sems):
    edge = conf_buf.shape[2]
    pairs = head_ref[0]

    def copies(p, slot):
        return [
            pltpu.make_async_copy(conf_ref.at[tile_ref[2 * p + k]], conf_buf.at[slot, k], sems.at[slot, k])
            for k in range(2)
        ]

    def fetch(p, slot):
        for c in copies(p, slot):
            c.start()

    for s in range(SLOTS):
        @pl.when(s < pairs)
        def _():
            fetch(s, s)

    item_gram = dot(items_ref[...], items_ref[...], 0, 0)
    user_gram = dot(users_ref[...], users_ref[...], 0, 0)
    high, low = split(GRAM_WEIGHT * item_gram)
    user_out[...] = dot(users_ref[...], high, 1, 0) + dot(users_ref[...], low, 1, 0)
    high, low = split(GRAM_WEIGHT * user_gram)
    item_out[...] = dot(items_ref[...], high, 1, 0) + dot(items_ref[...], low, 1, 0)

    def visit(p, carry):
        slot = lax.rem(p, SLOTS)
        u = pl.multiple_of(pair_ref[p] * edge, edge)
        v0 = pl.multiple_of(panel_ref[2 * p] * edge, edge)
        v1 = pl.multiple_of(panel_ref[2 * p + 1] * edge, edge)
        users = users_ref[pl.ds(u, edge), :]
        items = jnp.concatenate([items_ref[pl.ds(v0, edge), :], items_ref[pl.ds(v1, edge), :]], axis=0)
        scores = dot(users, items, 1, 1)
        for c in copies(p, slot):
            c.wait()
        left = conf_buf[slot, 0].astype(jnp.float32) * factor_ref[2 * p] * (scores[:, :edge] - 1.0)
        right = conf_buf[slot, 1].astype(jnp.float32) * factor_ref[2 * p + 1] * (scores[:, edge:] - 1.0)

        @pl.when(p + SLOTS < pairs)
        def _():
            fetch(p + SLOTS, slot)

        weighted = jnp.concatenate([left, right], axis=1).astype(jnp.bfloat16)
        user_out[pl.ds(u, edge), :] += dot(weighted, items, 1, 0)
        item_terms = dot(weighted, users, 0, 0)
        item_out[pl.ds(v0, edge), :] += item_terms[:edge]
        item_out[pl.ds(v1, edge), :] += item_terms[edge:]
        return carry

    lax.fori_loop(0, pairs, visit, 0)


def smem():
    return pl.BlockSpec(memory_space=pltpu.SMEM)


def vmem():
    return pl.BlockSpec(memory_space=pltpu.VMEM)


def local(user_factors, item_factors, confidence, tile_counts, tile_user, tile_item, block_slot, live_tiles):
    rows, rank = user_factors.shape
    tiles, edge = confidence.shape[2:4]
    blocks = rows // edge
    pairs = (tiles + blocks) // 2
    scale = jnp.log1p(tile_counts[0, 0].astype(jnp.float32))
    i32 = jnp.int32
    plan = pl.pallas_call(
        plan_kernel,
        out_shape=(
            jax.ShapeDtypeStruct((1,), i32),
            jax.ShapeDtypeStruct((pairs,), i32),
            jax.ShapeDtypeStruct((2 * pairs,), i32),
            jax.ShapeDtypeStruct((2 * pairs,), i32),
            jax.ShapeDtypeStruct((2 * pairs,), jnp.float32),
        ),
        in_specs=[smem()] * 5,
        out_specs=[smem()] * 5,
        scratch_shapes=[pltpu.SMEM((blocks,), i32)],
        name="plan",
    )(tile_user[0, 0], tile_item[0, 0], block_slot[0], live_tiles[0], scale)
    items = lax.all_gather(item_factors, "users", axis=1, tiled=True)[0]
    user_part, item_part = pl.pallas_call(
        tile_kernel,
        out_shape=(
            jax.ShapeDtypeStruct((rows, rank), jnp.float32),
            jax.ShapeDtypeStruct(items.shape, jnp.float32),
        ),
        in_specs=[smem()] * 5 + [vmem(), vmem(), pl.BlockSpec(memory_space=pl.ANY)],
        out_specs=[vmem(), vmem()],
        scratch_shapes=[pltpu.VMEM((SLOTS, 2, edge, edge), jnp.bfloat16), pltpu.SemaphoreType.DMA((SLOTS, 2))],
        name="tiles",
    )(*plan, user_factors, items, confidence[0, 0])
    user_grad = GRAD_SCALE * lax.psum(user_part, "items")
    item_grad = GRAD_SCALE * lax.psum_scatter(item_part, "users", scatter_dimension=0, tiled=True)
    return user_grad, item_grad[None]


def solution(mesh):
    in_specs = (
        P("users", None),
        P("items", "users", None),
        P("users", "items", None, None, None),
        P("users", "items", None),
        P("users", "items", None),
        P("users", "items", None),
        P("items", None),
        P("users", "items"),
    )
    out_specs = (P("users", None), P("items", "users", None))
    return jax.shard_map(local, mesh=mesh, in_specs=in_specs, out_specs=out_specs, check_vma=False)
```

```python
import jax
import jax.numpy as jnp
from jax import lax
from jax.experimental import pallas as pl
from jax.experimental.pallas import tpu as pltpu
from jax.sharding import PartitionSpec as P

GRAD_SCALE = 0.005
GRAM_WEIGHT = 0.5
SLOTS = 8
RING = 4
TAIL = 16
TOP = 32000.0


def dot(a, b, ca, cb):
    return lax.dot_general(a, b, (((ca,), (cb,)), ((), ())), preferred_element_type=jnp.float32)


def split(x):
    high = x.astype(jnp.bfloat16)
    return high, (x - high.astype(jnp.float32)).astype(jnp.bfloat16)


def encode(out_ref, x):
    rows = x.shape[0]
    top = jnp.max(jnp.abs(x), axis=0, keepdims=True)
    power = jnp.ceil(jnp.log2(jnp.maximum(top, 1e-30) * (1.0 / TOP)))
    out_ref[:rows, :] = jnp.round(x * jnp.exp2(-power)).astype(jnp.int32).astype(jnp.int16)
    tail = jnp.broadcast_to(power, (TAIL, x.shape[1]))
    out_ref[rows:, :] = tail.astype(jnp.int32).astype(jnp.int16)


def decode(ref):
    rows = ref.shape[0] - TAIL
    power = ref[rows:, :].astype(jnp.int32).astype(jnp.float32)[:1]
    return ref[:rows, :].astype(jnp.int32).astype(jnp.float32) * jnp.exp2(power)


def plan_kernel(here_ref, user_ref, item_ref, slot_ref, live_ref, scale_ref, head_ref, pair_ref, tile_ref, panel_ref, factor_ref, place_ref):
    user_total = place_ref.shape[0]
    pair_total = pair_ref.shape[0]
    live = live_ref[0]
    z = here_ref[0] // 8
    x = (here_ref[0] // 2) % RING
    core = here_ref[0] % 2

    def clear_user(u, carry):
        place_ref[u] = 0
        return carry

    lax.fori_loop(0, user_total, clear_user, 0)

    def clear_pair(p, carry):
        tile_ref[p] = 0
        panel_ref[p] = 0
        factor_ref[p] = 0.0
        return carry

    lax.fori_loop(0, 2 * pair_total, clear_pair, 0)

    def count(t, carry):
        u = user_ref[t]
        place_ref[u] = place_ref[u] + 1
        return carry

    lax.fori_loop(0, live, count, 0)

    def start(u, first):
        pairs = (place_ref[u] + 1) // 2
        place_ref[u] = 2 * first

        def name(p, carry):
            pair_ref[p] = u
            return carry

        lax.fori_loop(first, first + pairs, name, 0)
        return first + pairs

    head_ref[0] = lax.fori_loop(0, user_total, start, 0)
    head_ref[1] = here_ref[1]

    def put(t, carry):
        u = user_ref[t]
        spot = place_ref[u]
        place_ref[u] = spot + 1
        tile_ref[spot] = t
        s = slot_ref[item_ref[t]]
        far_core = (core + s) & 1
        far_z = (z - (s >> 3)) & 3
        far_x = (x - (s >> 1)) & 3
        panel_ref[spot] = far_core * 16 + far_z * 4 + far_x
        factor_ref[spot] = scale_ref[t]
        return carry

    lax.fori_loop(0, live, put, 0)


def tile_kernel(*refs):
    head_ref, pair_ref, tile_ref, panel_ref, factor_ref, users_ref, conf_ref = refs[:7]
    piece_refs = refs[7:23]
    user_own, user_1, user_2, user_3, item_own, item_0, item_1, item_2, item_3 = refs[23:32]
    items_ref, user_acc, item_acc, conf_buf, sems, piece_sems = refs[32:]
    edge = conf_buf.shape[2]
    rank = users_ref.shape[1]
    pairs = head_ref[0]
    y = head_ref[1]

    loads = []
    for i, piece in enumerate(piece_refs):
        core, half, k = i // 8, (i // 4) % 2, i % 4
        for j in range(RING):
            spot = core * 16 + (k * 4 + j if half == 0 else j * 4 + k)
            loads.append(pltpu.make_async_copy(piece.at[j], items_ref.at[spot, half], piece_sems.at[4 * i + j]))
    for c in loads:
        c.start()

    def copies(p, slot):
        return [
            pltpu.make_async_copy(conf_ref.at[tile_ref[2 * p + k]], conf_buf.at[slot, k], sems.at[slot, k])
            for k in range(2)
        ]

    def fetch(p, slot):
        for c in copies(p, slot):
            c.start()

    for s in range(SLOTS):
        @pl.when(s < pairs)
        def _():
            fetch(s, s)

    user_gram = dot(users_ref[...], users_ref[...], 0, 0)
    for c in loads:
        c.wait()
    every = items_ref[...].reshape(-1, rank)
    item_gram = dot(every, every, 0, 0)
    high, low = split(GRAM_WEIGHT * item_gram)
    quarter = user_acc.shape[0] // RING
    for k in range(RING):
        q = pl.multiple_of(((y - k) & 3) * quarter, quarter)
        rows = users_ref[pl.ds(q, quarter), :]
        user_acc[k * quarter:(k + 1) * quarter, :] = dot(rows, high, 1, 0) + dot(rows, low, 1, 0)
    high, low = split(GRAM_WEIGHT * user_gram)
    item_acc[...] = dot(every, high, 1, 0) + dot(every, low, 1, 0)

    def visit(p, carry):
        slot = lax.rem(p, SLOTS)
        b = pair_ref[p]
        u = pl.multiple_of(b * edge, edge)
        r = pl.multiple_of(((((y - (b >> 2)) & 3) << 2) + (b & 3)) * edge, edge)
        v0 = panel_ref[2 * p]
        v1 = panel_ref[2 * p + 1]
        users = users_ref[pl.ds(u, edge), :]
        items = jnp.concatenate([items_ref[v0].reshape(edge, rank), items_ref[v1].reshape(edge, rank)], axis=0)
        scores = dot(users, items, 1, 1)
        for c in copies(p, slot):
            c.wait()
        left = conf_buf[slot, 0].astype(jnp.float32) * factor_ref[2 * p] * (scores[:, :edge] - 1.0)
        right = conf_buf[slot, 1].astype(jnp.float32) * factor_ref[2 * p + 1] * (scores[:, edge:] - 1.0)

        @pl.when(p + SLOTS < pairs)
        def _():
            fetch(p + SLOTS, slot)

        weighted = jnp.concatenate([left, right], axis=1).astype(jnp.bfloat16)
        user_acc[pl.ds(r, edge), :] += dot(weighted, items, 1, 0)
        item_terms = dot(weighted, users, 0, 0)
        r0 = pl.multiple_of(v0 * edge, edge)
        r1 = pl.multiple_of(v1 * edge, edge)
        item_acc[pl.ds(r0, edge), :] += item_terms[:edge]
        item_acc[pl.ds(r1, edge), :] += item_terms[edge:]
        return carry

    lax.fori_loop(0, pairs, visit, 0)
    user_own[...] = user_acc[:quarter, :]
    for k, out in enumerate((user_1, user_2, user_3)):
        encode(out, user_acc[(k + 1) * quarter:(k + 2) * quarter, :])
    half = item_acc.shape[0] // 2
    item_own[...] = item_acc[:half, :]
    part = half // RING
    for k, out in enumerate((item_0, item_1, item_2, item_3)):
        encode(out, item_acc[half + k * part:half + (k + 1) * part, :])


def user_sum_kernel(own_ref, p1, p2, p3, out_ref):
    encode(out_ref, (own_ref[...] + decode(p1)) + (decode(p2) + decode(p3)))


def user_out_kernel(here_ref, p0, p1, p2, p3, out_ref):
    quarter = p0.shape[0] - TAIL
    for k, p in enumerate((p0, p1, p2, p3)):
        q = pl.multiple_of(((here_ref[1] - k) & 3) * quarter, quarter)
        out_ref[pl.ds(q, quarter), :] = GRAD_SCALE * decode(p)


def item_core_kernel(own_ref, c0, c1, c2, c3, za, z1, z2, z3, xa, x1, x2, x3, acc):
    part = own_ref.shape[0] // RING
    rank = own_ref.shape[1]
    for k, c in enumerate((c0, c1, c2, c3)):
        acc[k] = (own_ref[k * part:(k + 1) * part, :] + decode(c)).reshape(acc.shape[1:])
    for k, out in enumerate((za, z1, z2, z3)):
        rows = acc[k, :, 0].reshape(-1, rank)
        if k == 0:
            out[...] = rows
        else:
            encode(out, rows)
    for k, out in enumerate((xa, x1, x2, x3)):
        rows = acc[:, k, 1].reshape(-1, rank)
        if k == 0:
            out[...] = rows
        else:
            encode(out, rows)


def item_mid_kernel(za, z1, z2, z3, xa, x1, x2, x3, o0, o1, o2, o3, q0, q1, q2, q3):
    for ins, outs in (((za, z1, z2, z3), (o0, o1, o2, o3)), ((xa, x1, x2, x3), (q0, q1, q2, q3))):
        total = (ins[0][...] + decode(ins[1])) + (decode(ins[2]) + decode(ins[3]))
        rows = total.shape[0] // RING
        for k, out in enumerate(outs):
            out[...] = total[k * rows:(k + 1) * rows]


def item_out_kernel(o0, o1, o2, o3, q0, q1, q2, q3, out_ref):
    rows = o0.shape[0]
    out_ref[:rows, :] = GRAD_SCALE * ((o0[...] + o1[...]) + (o2[...] + o3[...]))
    out_ref[rows:, :] = GRAD_SCALE * ((q0[...] + q1[...]) + (q2[...] + q3[...]))


def smem():
    return pl.BlockSpec(memory_space=pltpu.SMEM)


def vmem():
    return pl.BlockSpec(memory_space=pltpu.VMEM)


def anywhere():
    return pl.BlockSpec(memory_space=pl.ANY)


def f32(*shape):
    return jax.ShapeDtypeStruct(shape, jnp.float32)


def i32(*shape):
    return jax.ShapeDtypeStruct(shape, jnp.int32)


def i16(*shape):
    return jax.ShapeDtypeStruct(shape, jnp.int16)


def local(user_factors, item_factors, confidence, tile_counts, tile_user, tile_item, block_slot, live_tiles):
    rows, rank = user_factors.shape
    tiles, edge = confidence.shape[2:4]
    blocks = rows // edge
    pairs = (tiles + blocks) // 2
    users_size = lax.axis_size("users")
    items_size = lax.axis_size("items")
    spots = range(users_size)

    def along_y(a, k):
        return lax.ppermute(a, "items", [(i, (i + k) % items_size) for i in range(items_size)])

    def along_x(a, k):
        return lax.ppermute(a, "users", [(i, (i // 8) * 8 + (i // 2 + k) % 4 * 2 + i % 2) for i in spots])

    def along_z(a, k):
        return lax.ppermute(a, "users", [(i, (i // 8 + k) % 4 * 8 + i % 8) for i in spots])

    def to_core(a):
        return lax.ppermute(a, "users", [(i, i ^ 1) for i in spots])

    where = lax.broadcasted_iota(jnp.int32, (2,), 0)
    here = jnp.where(where == 0, lax.axis_index("users"), lax.axis_index("items")).astype(jnp.int32)

    own = item_factors[0].reshape(2, edge // 2, rank)
    first_x = jnp.stack([own[0]] + [along_x(own[0], k) for k in (1, 2, 3)])
    first_z = jnp.stack([own[1]] + [along_z(own[1], k) for k in (1, 2, 3)])
    pieces = [first_x] + [along_z(first_x, k) for k in (1, 2, 3)]
    pieces += [first_z] + [along_x(first_z, k) for k in (1, 2, 3)]
    pieces += [to_core(a) for a in pieces]

    scale = jnp.log1p(tile_counts[0, 0].astype(jnp.float32))
    plan = pl.pallas_call(
        plan_kernel,
        out_shape=(i32(2), i32(pairs), i32(2 * pairs), i32(2 * pairs), f32(2 * pairs)),
        in_specs=[smem()] * 6,
        out_specs=[smem()] * 5,
        scratch_shapes=[pltpu.SMEM((blocks,), jnp.int32)],
        name="plan",
    )(here, tile_user[0, 0], tile_item[0, 0], block_slot[0], live_tiles[0], scale)

    quarter = rows // 4
    panels = users_size
    half_rows = panels * edge // 2
    part = half_rows // 4
    outs = pl.pallas_call(
        tile_kernel,
        out_shape=(f32(quarter, rank),) + (i16(quarter + TAIL, rank),) * 3 + (f32(half_rows, rank),) + (i16(part + TAIL, rank),) * 4,
        in_specs=[smem()] * 5 + [vmem(), anywhere()] + [anywhere()] * 16,
        out_specs=[vmem()] * 9,
        scratch_shapes=[
            pltpu.VMEM((panels, 2, edge // 2, rank), jnp.bfloat16),
            pltpu.VMEM((rows, rank), jnp.float32),
            pltpu.VMEM((panels * edge, rank), jnp.float32),
            pltpu.VMEM((SLOTS, 2, edge, edge), jnp.bfloat16),
            pltpu.SemaphoreType.DMA((SLOTS, 2)),
            pltpu.SemaphoreType.DMA((64,)),
        ],
        name="tiles",
    )(*plan, user_factors, confidence[0, 0], *pieces)
    user_own, user_parts, item_own, item_parts = outs[0], outs[1:4], outs[4], outs[5:9]

    user_parts = [along_y(a, -k) for k, a in zip((1, 2, 3), user_parts)]
    item_parts = [to_core(a) for a in item_parts]

    piece = (i16(half_rows // 8 + TAIL, rank),) * 3
    whole = (f32(half_rows // 8, rank),)
    mids = pl.pallas_call(
        item_core_kernel,
        out_shape=whole + piece + whole + piece,
        in_specs=[vmem()] * 5,
        out_specs=[vmem()] * 8,
        scratch_shapes=[pltpu.VMEM((4, 4, 2, edge // 2, rank), jnp.float32)],
        name="item_core",
    )(item_own, *item_parts)
    mids = list(mids)
    for k in (1, 2, 3):
        mids[k] = along_z(mids[k], -k)
        mids[4 + k] = along_x(mids[4 + k], -k)

    user_code = pl.pallas_call(
        user_sum_kernel,
        out_shape=i16(quarter + TAIL, rank),
        in_specs=[vmem()] * 4,
        out_specs=vmem(),
        name="user_sum",
    )(user_own, *user_parts)
    user_codes = [user_code] + [along_y(user_code, k) for k in (1, 2, 3)]

    ends = pl.pallas_call(
        item_mid_kernel,
        out_shape=(f32(edge // 2, rank),) * 8,
        in_specs=[vmem()] * 8,
        out_specs=[vmem()] * 8,
        name="item_mid",
    )(*mids)
    ends = list(ends)
    for k in (1, 2, 3):
        ends[k] = along_x(ends[k], -k)
        ends[4 + k] = along_z(ends[4 + k], -k)
    item_grad = pl.pallas_call(
        item_out_kernel,
        out_shape=f32(edge, rank),
        in_specs=[vmem()] * 8,
        out_specs=vmem(),
        name="item_out",
    )(*ends)
    user_grad = pl.pallas_call(
        user_out_kernel,
        out_shape=f32(rows, rank),
        in_specs=[smem()] + [vmem()] * 4,
        out_specs=vmem(),
        name="user_out",
    )(here, *user_codes)
    return user_grad, item_grad[None]


def solution(mesh):
    in_specs = (
        P("users", None),
        P("items", "users", None),
        P("users", "items", None, None, None),
        P("users", "items", None),
        P("users", "items", None),
        P("users", "items", None),
        P("items", None),
        P("users", "items"),
    )
    out_specs = (P("users", None), P("items", "users", None))
    return jax.shard_map(local, mesh=mesh, in_specs=in_specs, out_specs=out_specs, check_vma=False)
```

```python
import jax
import jax.numpy as jnp
from jax import lax
from jax.experimental import pallas as pl
from jax.experimental.pallas import tpu as pltpu
from jax.sharding import PartitionSpec as P

GRAD_SCALE = 0.005
GRAM_WEIGHT = 0.5
SLOTS = 8
GROUP = 4
RING = 4
TAIL = 16
TOP = 32000.0


def dot(a, b, ca, cb):
    return lax.dot_general(a, b, (((ca,), (cb,)), ((), ())), preferred_element_type=jnp.float32)


def split(x):
    high = x.astype(jnp.bfloat16)
    return high, (x - high.astype(jnp.float32)).astype(jnp.bfloat16)


def encode(out_ref, x):
    rows = x.shape[0]
    top = jnp.max(jnp.abs(x), axis=0, keepdims=True)
    power = jnp.ceil(jnp.log2(jnp.maximum(top, 1e-30) * (1.0 / TOP)))
    out_ref[:rows, :] = jnp.round(x * jnp.exp2(-power)).astype(jnp.int32).astype(jnp.int16)
    tail = jnp.broadcast_to(power, (TAIL, x.shape[1]))
    out_ref[rows:, :] = tail.astype(jnp.int32).astype(jnp.int16)


def decode(ref):
    rows = ref.shape[0] - TAIL
    power = ref[rows:, :].astype(jnp.int32).astype(jnp.float32)[:1]
    return ref[:rows, :].astype(jnp.int32).astype(jnp.float32) * jnp.exp2(power)


def plan_kernel(here_ref, live_ref, user_ref, item_ref, count_ref, slot_ref, head_ref, pair_ref, tile_ref, panel_ref, factor_ref):
    tiles = user_ref.shape[1]
    spots = tile_ref.shape[1]
    panels = slot_ref.shape[1]
    z = here_ref[0] // 8
    x = (here_ref[0] // 2) & 3
    core = here_ref[0] & 1

    def grid(rows, lanes, axis):
        return lax.broadcasted_iota(jnp.int32, (rows, lanes), axis)

    down = grid(tiles, tiles, 0)
    across = grid(tiles, tiles, 1)

    def pick(mask, values, axis):
        return jnp.sum(jnp.where(mask, values, 0.0), axis=axis, keepdims=True)

    def column(row):
        return pick(down == across, row.astype(jnp.float32), 1)

    user_row = user_ref[...]
    user = column(user_row)
    user_int = user.astype(jnp.int32)
    order = grid(tiles, 1, 0)
    used = order < live_ref[0]
    rank = pick((user_int == user_row) & (across < down), jnp.ones((1, 1), jnp.float32), 1)
    own = (user_int == grid(tiles, 128, 1)) & used
    sizes = pick(own, jnp.ones((1, 1), jnp.float32), 0).astype(jnp.int32)
    groups = ((sizes + (GROUP - 1)) // GROUP).astype(jnp.float32)
    first = pick(grid(tiles, 128, 1) < user_int, groups, 1)
    spot = jnp.where(used, GROUP * first + rank, -1.0).astype(jnp.int32)
    item = column(item_ref[...]).astype(jnp.int32)
    slot = pick(item == grid(tiles, panels, 1), slot_ref[...].astype(jnp.float32), 1).astype(jnp.int32)
    far_z = (z - (slot >> 3)) & 3
    far_x = (x - (slot >> 1)) & 3
    odd = (slot & 1) == 1
    panel = ((core + slot) & 1) * 16 + jnp.where(odd, far_z * 4 + far_x, far_x * 4 + far_z)
    factor = jnp.log(1.0 + column(count_ref[...]))
    at = spot == grid(tiles, spots, 1)
    tile_ref[...] = pick(at, order.astype(jnp.float32), 0).astype(jnp.int32)
    panel_ref[...] = pick(at, panel.astype(jnp.float32), 0).astype(jnp.int32)
    factor_ref[...] = pick(at, factor, 0)
    pair_ref[...] = pick(spot == GROUP * grid(tiles, pair_ref.shape[1], 1), user, 0).astype(jnp.int32)
    total = jnp.sum(groups, axis=1, keepdims=True).astype(jnp.int32)
    head_ref[...] = jnp.where(grid(1, 128, 1) == 0, total, here_ref[1])


def tile_kernel(*refs):
    head_ref, pair_ref, tile_ref, panel_ref, factor_ref, users_ref, conf_ref = refs[:7]
    piece_refs = refs[7:15]
    user_own, user_1, user_2, user_3, item_own, item_0, item_1, item_2, item_3 = refs[15:24]
    items_ref, user_acc, item_acc, conf_buf, weights_ref, sems, piece_sems = refs[24:]
    edge = conf_buf.shape[2]
    rank = users_ref.shape[1]
    groups = head_ref[0, 0]
    y = head_ref[0, 1]

    loads = [
        pltpu.make_async_copy(piece, items_ref.at[pl.ds(RING * i, RING)], piece_sems.at[i])
        for i, piece in enumerate(piece_refs)
    ]
    for c in loads:
        c.start()

    def copies(p, slot):
        return [
            pltpu.make_async_copy(conf_ref.at[tile_ref[0, GROUP * p + k]], conf_buf.at[slot, k], sems.at[slot, k])
            for k in range(GROUP)
        ]

    def fetch(p, slot):
        for c in copies(p, slot):
            c.start()

    for s in range(SLOTS):
        @pl.when(s <= groups)
        def _():
            fetch(s, s)

    user_gram = dot(users_ref[...], users_ref[...], 0, 0)
    for c in loads:
        c.wait()
    every = items_ref[...].reshape(-1, rank)
    item_gram = dot(every, every, 0, 0)
    high, low = split(GRAM_WEIGHT * item_gram)
    quarter = user_acc.shape[0] // RING
    for k in range(RING):
        q = pl.multiple_of(((y - k) & 3) * quarter, quarter)
        rows = users_ref[pl.ds(q, quarter), :]
        user_acc[k * quarter:(k + 1) * quarter, :] = dot(rows, high, 1, 0) + dot(rows, low, 1, 0)
    high, low = split(GRAM_WEIGHT * user_gram)
    item_acc[...] = dot(every, high, 1, 0) + dot(every, low, 1, 0)

    def prepare(g):
        slot = lax.rem(g, SLOTS)
        u = pl.multiple_of(pair_ref[0, g] * edge, edge)
        users = users_ref[pl.ds(u, edge), :]
        scores = []
        for j in range(GROUP // 2):
            v0 = panel_ref[0, GROUP * g + 2 * j]
            v1 = panel_ref[0, GROUP * g + 2 * j + 1]
            items = jnp.concatenate([items_ref[v0], items_ref[v1]], axis=0)
            scores.append(dot(users, items, 1, 1))
        for c in copies(g, slot):
            c.wait()
        for k in range(GROUP):
            part = scores[k // 2][:, (k % 2) * edge:(k % 2 + 1) * edge]
            weight = conf_buf[slot, k].astype(jnp.float32) * factor_ref[0, GROUP * g + k] * (part - 1.0)
            weights_ref[:, k * edge:(k + 1) * edge] = weight.astype(jnp.bfloat16)

        @pl.when(g + SLOTS <= groups)
        def _():
            fetch(g + SLOTS, slot)

    prepare(0)

    def visit(g, carry):
        b = pair_ref[0, g]
        u = pl.multiple_of(b * edge, edge)
        r = pl.multiple_of(((((y - (b >> 2)) & 3) << 2) + (b & 3)) * edge, edge)
        spots = [panel_ref[0, GROUP * g + k] for k in range(GROUP)]
        users = users_ref[pl.ds(u, edge), :]
        items = jnp.concatenate([items_ref[v] for v in spots], axis=0)
        weights = weights_ref[...]
        user_terms = dot(weights, items, 1, 0)
        item_terms = dot(weights, users, 0, 0)
        prepare(g + 1)
        user_acc[pl.ds(r, edge), :] += user_terms
        for k, v in enumerate(spots):
            rk = pl.multiple_of(v * edge, edge)
            item_acc[pl.ds(rk, edge), :] += item_terms[k * edge:(k + 1) * edge]
        return carry

    lax.fori_loop(0, groups, visit, 0)
    user_own[...] = user_acc[:quarter, :]
    for k, out in enumerate((user_1, user_2, user_3)):
        encode(out, user_acc[(k + 1) * quarter:(k + 2) * quarter, :])
    half = item_acc.shape[0] // 2
    item_own[...] = item_acc[:half, :]
    part = half // RING
    for k, out in enumerate((item_0, item_1, item_2, item_3)):
        encode(out, item_acc[half + k * part:half + (k + 1) * part, :])


def user_sum_kernel(after_ref, own_ref, p1, p2, p3, out_ref):
    encode(out_ref, (own_ref[...] + decode(p1)) + (decode(p2) + decode(p3)))


def user_out_kernel(here_ref, p0, p1, p2, p3, out_ref):
    quarter = p0.shape[0] - TAIL
    for k, p in enumerate((p0, p1, p2, p3)):
        q = pl.multiple_of(((here_ref[1] - k) & 3) * quarter, quarter)
        out_ref[pl.ds(q, quarter), :] = GRAD_SCALE * decode(p)


def item_core_kernel(own_ref, c0, c1, c2, c3, own_out, p1, p2, p3):
    part = own_out.shape[0]
    own_out[...] = own_ref[:part, :] + decode(c0)
    for k, (c, out) in enumerate(((c1, p1), (c2, p2), (c3, p3))):
        encode(out, own_ref[(k + 1) * part:(k + 2) * part, :] + decode(c))


def item_mid_kernel(own_ref, c1, c2, c3, own_out, p1, p2, p3):
    part = own_out.shape[0]
    total = (own_ref[...] + decode(c1)) + (decode(c2) + decode(c3))
    own_out[...] = total[:part]
    for k, out in enumerate((p1, p2, p3)):
        encode(out, total[(k + 1) * part:(k + 2) * part])


def item_out_kernel(own_ref, p1, p2, p3, out_ref):
    out_ref[...] = GRAD_SCALE * ((own_ref[...] + decode(p1)) + (decode(p2) + decode(p3)))


def smem():
    return pl.BlockSpec(memory_space=pltpu.SMEM)


def vmem():
    return pl.BlockSpec(memory_space=pltpu.VMEM)


def anywhere():
    return pl.BlockSpec(memory_space=pl.ANY)


def f32(*shape):
    return jax.ShapeDtypeStruct(shape, jnp.float32)


def i32(*shape):
    return jax.ShapeDtypeStruct(shape, jnp.int32)


def i16(*shape):
    return jax.ShapeDtypeStruct(shape, jnp.int16)


def local(user_factors, item_factors, confidence, tile_counts, tile_user, tile_item, block_slot, live_tiles):
    rows, rank = user_factors.shape
    tiles, edge = confidence.shape[2:4]
    blocks = rows // edge
    pairs = (tiles + (GROUP - 1) * blocks) // GROUP + 1
    users_size = lax.axis_size("users")
    items_size = lax.axis_size("items")
    spots = range(users_size)

    def along_y(a, k):
        return lax.ppermute(a, "items", [(i, (i + k) % items_size) for i in range(items_size)])

    def move(i, by_z, k):
        z, x, core = i // 8, i // 2 % 4, i % 2
        if by_z:
            z = (z + k) % 4
        else:
            x = (x + k) % 4
        return z * 8 + x * 2 + core

    def along_first(a, k):
        return lax.ppermute(a, "users", [(i, move(i, i % 2 == 0, k)) for i in spots])

    def along_second(a, k):
        return lax.ppermute(a, "users", [(i, move(i, i % 2 == 1, k)) for i in spots])

    def to_core(a):
        return lax.ppermute(a, "users", [(i, i ^ 1) for i in spots])

    where = lax.broadcasted_iota(jnp.int32, (2,), 0)
    here = jnp.where(where == 0, lax.axis_index("users"), lax.axis_index("items")).astype(jnp.int32)

    own = item_factors[0]
    first = [own] + [along_first(own, k) for k in (1, 2, 3)]
    spot_total = -(-(GROUP * pairs) // 128) * 128
    plan = pl.pallas_call(
        plan_kernel,
        out_shape=(i32(1, 128), i32(1, 128), i32(1, spot_total), i32(1, spot_total), f32(1, spot_total)),
        in_specs=[smem()] * 2 + [vmem()] * 4,
        out_specs=[vmem()] * 5,
        name="plan",
    )(here, live_tiles[0], tile_user[0], tile_item[0], tile_counts[0], block_slot)
    first = jnp.stack(first)
    first, plan = lax.optimization_barrier((first, plan))
    pieces = [first] + [along_second(first, k) for k in (1, 2, 3)]
    pieces += [to_core(a) for a in pieces]

    quarter = rows // 4
    panels = users_size
    half_rows = panels * edge // 2
    part = half_rows // 4
    outs = pl.pallas_call(
        tile_kernel,
        out_shape=(f32(quarter, rank),) + (i16(quarter + TAIL, rank),) * 3 + (f32(half_rows, rank),) + (i16(part + TAIL, rank),) * 4,
        in_specs=[smem()] * 5 + [vmem(), anywhere()] + [anywhere()] * 8,
        out_specs=[vmem()] * 9,
        scratch_shapes=[
            pltpu.VMEM((panels, edge, rank), jnp.bfloat16),
            pltpu.VMEM((rows, rank), jnp.float32),
            pltpu.VMEM((panels * edge, rank), jnp.float32),
            pltpu.VMEM((SLOTS, GROUP, edge, edge), jnp.bfloat16),
            pltpu.VMEM((edge, GROUP * edge), jnp.bfloat16),
            pltpu.SemaphoreType.DMA((SLOTS, GROUP)),
            pltpu.SemaphoreType.DMA((8,)),
        ],
        name="tiles",
    )(*plan, user_factors, confidence[0, 0], *pieces)
    user_own, user_parts, item_own, item_parts = outs[0], outs[1:4], outs[4], outs[5:9]

    item_parts = [to_core(a) for a in item_parts]
    user_parts = [along_y(a, -k) for k, a in zip((1, 2, 3), user_parts)]

    def item_stage(kernel, name, size, *ins):
        return pl.pallas_call(
            kernel,
            out_shape=(f32(size, rank),) + (i16(size + TAIL, rank),) * 3,
            in_specs=[vmem()] * len(ins),
            out_specs=[vmem()] * 4,
            name=name,
        )(*ins)

    item_own, *item_parts = item_stage(item_core_kernel, "item_core", part, item_own, *item_parts)
    after = item_own
    item_parts = [along_second(a, -k) for k, a in zip((1, 2, 3), item_parts)]
    user_code = pl.pallas_call(
        user_sum_kernel,
        out_shape=i16(quarter + TAIL, rank),
        in_specs=[anywhere()] + [vmem()] * 4,
        out_specs=vmem(),
        name="user_sum",
    )(after, user_own, *user_parts)
    user_codes = [user_code] + [along_y(user_code, k) for k in (1, 2, 3)]
    item_own, *item_parts = item_stage(item_mid_kernel, "item_mid", edge, item_own, *item_parts)
    item_parts = [along_first(a, -k) for k, a in zip((1, 2, 3), item_parts)]
    item_grad = pl.pallas_call(
        item_out_kernel,
        out_shape=f32(edge, rank),
        in_specs=[vmem()] * 4,
        out_specs=vmem(),
        name="item_out",
    )(item_own, *item_parts)
    user_grad = pl.pallas_call(
        user_out_kernel,
        out_shape=f32(rows, rank),
        in_specs=[smem()] + [vmem()] * 4,
        out_specs=vmem(),
        name="user_out",
    )(here, *user_codes)
    return user_grad, item_grad[None]


def solution(mesh):
    in_specs = (
        P("users", None),
        P("items", "users", None),
        P("users", "items", None, None, None),
        P("users", "items", None),
        P("users", "items", None),
        P("users", "items", None),
        P("items", None),
        P("users", "items"),
    )
    out_specs = (P("users", None), P("items", "users", None))
    return jax.shard_map(local, mesh=mesh, in_specs=in_specs, out_specs=out_specs, check_vma=False)
```

```python
import jax
import jax.numpy as jnp
from jax import lax
from jax.experimental import pallas as pl
from jax.experimental.pallas import tpu as pltpu
from jax.sharding import PartitionSpec as P

GRAD_SCALE = 0.005
GRAM_WEIGHT = 0.5
SLOTS = 8
GROUP = 4
UNROLL = 2
RING = 4
TAIL = 16
TOP = 32000.0


def dot(a, b, ca, cb):
    return lax.dot_general(a, b, (((ca,), (cb,)), ((), ())), preferred_element_type=jnp.float32)


def split(x):
    high = x.astype(jnp.bfloat16)
    return high, (x - high.astype(jnp.float32)).astype(jnp.bfloat16)


def encode(out_ref, x):
    rows = x.shape[0]
    top = jnp.max(jnp.abs(x), axis=0, keepdims=True)
    power = jnp.ceil(jnp.log2(jnp.maximum(top, 1e-30) * (1.0 / TOP)))
    out_ref[:rows, :] = jnp.round(x * jnp.exp2(-power)).astype(jnp.int32).astype(jnp.int16)
    tail = jnp.broadcast_to(power, (TAIL, x.shape[1]))
    out_ref[rows:, :] = tail.astype(jnp.int32).astype(jnp.int16)


def decode(ref):
    rows = ref.shape[0] - TAIL
    power = ref[rows:, :].astype(jnp.int32).astype(jnp.float32)[:1]
    return ref[:rows, :].astype(jnp.int32).astype(jnp.float32) * jnp.exp2(power)


def plan_kernel(here_ref, live_ref, user_ref, item_ref, count_ref, slot_ref, head_ref, pair_ref, tile_ref, panel_ref, factor_ref, group_ref, weight_ref, block_ref):
    tiles = user_ref.shape[1]
    spots = tile_ref.shape[1]
    panels = slot_ref.shape[1]
    z = here_ref[0] // 8
    x = (here_ref[0] // 2) & 3
    core = here_ref[0] & 1

    def grid(rows, lanes, axis):
        return lax.broadcasted_iota(jnp.int32, (rows, lanes), axis)

    down = grid(tiles, tiles, 0)
    across = grid(tiles, tiles, 1)

    def pick(mask, values, axis):
        return jnp.sum(jnp.where(mask, values, 0.0), axis=axis, keepdims=True)

    def column(row):
        return pick(down == across, row.astype(jnp.float32), 1)

    user_row = user_ref[...]
    user = column(user_row)
    user_int = user.astype(jnp.int32)
    order = grid(tiles, 1, 0)
    used = order < live_ref[0]
    rank = pick((user_int == user_row) & (across < down), jnp.ones((1, 1), jnp.float32), 1)
    own = (user_int == grid(tiles, 128, 1)) & used
    sizes = pick(own, jnp.ones((1, 1), jnp.float32), 0).astype(jnp.int32)
    groups = ((sizes + (GROUP - 1)) // GROUP).astype(jnp.float32)
    first = pick(grid(tiles, 128, 1) < user_int, groups, 1)
    spot = jnp.where(used, GROUP * first + rank, -1.0).astype(jnp.int32)
    item = column(item_ref[...]).astype(jnp.int32)
    slot = pick(item == grid(tiles, panels, 1), slot_ref[...].astype(jnp.float32), 1).astype(jnp.int32)
    far_z = (z - (slot >> 3)) & 3
    far_x = (x - (slot >> 1)) & 3
    odd = (slot & 1) == 1
    panel = ((core + slot) & 1) * 16 + jnp.where(odd, far_z * 4 + far_x, far_x * 4 + far_z)
    factor = jnp.log(1.0 + column(count_ref[...]))
    at = spot == grid(tiles, spots, 1)
    tile_ref[...] = pick(at, order.astype(jnp.float32), 0).astype(jnp.int32)
    panel_ref[...] = pick(at, panel.astype(jnp.float32), 0).astype(jnp.int32)
    factor_ref[...] = pick(at, factor, 0)
    pair_ref[...] = pick(spot == GROUP * grid(tiles, pair_ref.shape[1], 1), user, 0).astype(jnp.int32)
    total = jnp.sum(groups, axis=1, keepdims=True)
    empty = GROUP * total
    panel_row = pick(down == across, panel.astype(jnp.float32), 0).astype(jnp.int32)
    rank = pick((panel == panel_row) & (across < down), jnp.ones((1, 1), jnp.float32), 1)
    own = (panel == grid(tiles, 128, 1)) & used
    sizes = pick(own, jnp.ones((1, 1), jnp.float32), 0).astype(jnp.int32)
    groups = ((sizes + (GROUP - 1)) // GROUP).astype(jnp.float32)
    first = pick(grid(tiles, 128, 1) < panel, groups, 1)
    place = jnp.where(used, GROUP * first + rank, -1.0).astype(jnp.int32)
    at = place == grid(tiles, spots, 1)
    weight_ref[...] = (pick(at, spot.astype(jnp.float32) - empty, 0) + empty).astype(jnp.int32)
    block_ref[...] = pick(at, user, 0).astype(jnp.int32)
    group_ref[...] = pick(place == GROUP * grid(tiles, 128, 1), panel.astype(jnp.float32), 0).astype(jnp.int32)
    lane = grid(1, 128, 1)
    item_total = jnp.sum(groups, axis=1, keepdims=True)
    numbers = jnp.where(lane == 0, total, item_total).astype(jnp.int32)
    rounded = (numbers + (UNROLL - 1)) // UNROLL * UNROLL
    head_ref[...] = jnp.where(lane == 1, here_ref[1], rounded)


def loads_of(piece_refs, items_ref, sems):
    return [
        pltpu.make_async_copy(piece, items_ref.at[pl.ds(RING * i, RING)], sems.at[i])
        for i, piece in enumerate(piece_refs)
    ]


def user_kernel(*refs):
    head_ref, pair_ref, tile_ref, panel_ref, factor_ref, users_ref, conf_ref = refs[:7]
    piece_refs = refs[7:15]
    user_own, user_1, user_2, user_3, weight_out = refs[15:20]
    items_ref, user_acc, conf_buf, weights_ref, sems, piece_sems, out_sems = refs[20:]
    edge = conf_buf.shape[2]
    rank = users_ref.shape[1]
    groups = head_ref[0, 0]
    y = head_ref[0, 1]

    loads = loads_of(piece_refs, items_ref, piece_sems)
    for c in loads:
        c.start()

    def fetch(p):
        slot = lax.rem(p, SLOTS)
        for k in range(GROUP):
            tile = tile_ref[0, GROUP * p + k]
            pltpu.make_async_copy(conf_ref.at[tile], conf_buf.at[slot, k], sems.at[slot]).start()

    def arrive(p):
        slot = lax.rem(p, SLOTS)
        pltpu.make_async_copy(conf_ref.at[pl.ds(0, GROUP)], conf_buf.at[slot], sems.at[slot]).wait()

    def leave(p):
        rows = pl.ds(GROUP * p, GROUP)
        return pltpu.make_async_copy(weights_ref.at[rows], weight_out.at[rows], out_sems.at[p])

    for s in range(SLOTS):
        fetch(s)

    item_gram = jnp.zeros((rank, rank), jnp.float32)
    for i, c in enumerate(loads):
        c.wait()
        rows = items_ref[RING * i:RING * (i + 1)].reshape(-1, rank)
        item_gram = item_gram + dot(rows, rows, 0, 0)
    high, low = split(GRAM_WEIGHT * item_gram)
    quarter = user_acc.shape[0] // RING
    for k in range(RING):
        q = pl.multiple_of(((y - k) & 3) * quarter, quarter)
        rows = users_ref[pl.ds(q, quarter), :]
        user_acc[k * quarter:(k + 1) * quarter, :] = dot(rows, high, 1, 0) + dot(rows, low, 1, 0)

    def prepare(g):
        slot = lax.rem(g, SLOTS)
        u = pl.multiple_of(pair_ref[0, g] * edge, edge)
        users = users_ref[pl.ds(u, edge), :]
        scores = []
        for j in range(GROUP // 2):
            v0 = panel_ref[0, GROUP * g + 2 * j]
            v1 = panel_ref[0, GROUP * g + 2 * j + 1]
            items = jnp.concatenate([items_ref[v0], items_ref[v1]], axis=0)
            scores.append(dot(users, items, 1, 1))
        for k in range(GROUP):
            part = scores[k // 2][:, (k % 2) * edge:(k % 2 + 1) * edge]
            weight = conf_buf[slot, k].astype(jnp.float32) * factor_ref[0, GROUP * g + k] * (part - 1.0)
            weights_ref[GROUP * g + k] = weight.astype(jnp.bfloat16)

    for j in range(UNROLL):
        arrive(j)
    for j in range(UNROLL):
        prepare(j)

    def visit(i, carry):
        base = i * UNROLL
        for j in range(UNROLL):
            arrive(base + UNROLL + j)
        for j in range(UNROLL):
            fetch(base + j + SLOTS)
            leave(base + j).start()
        terms = []
        for j in range(UNROLL):
            g = base + j
            items = jnp.concatenate([items_ref[panel_ref[0, GROUP * g + k]] for k in range(GROUP)], axis=0)
            weights = jnp.concatenate([weights_ref[GROUP * g + k] for k in range(GROUP)], axis=1)
            terms.append(dot(weights, items, 1, 0))
        for j in range(UNROLL):
            prepare(base + UNROLL + j)
        for j in range(UNROLL):
            b = pair_ref[0, base + j]
            r = pl.multiple_of(((((y - (b >> 2)) & 3) << 2) + (b & 3)) * edge, edge)
            user_acc[pl.ds(r, edge), :] += terms[j]
        return carry

    lax.fori_loop(0, groups // UNROLL, visit, 0)
    for j in range(UNROLL):
        leave(groups + j).start()
    for j in range(UNROLL, SLOTS):
        arrive(groups + j)
    user_own[...] = user_acc[:quarter, :]
    for k, out in enumerate((user_1, user_2, user_3)):
        encode(out, user_acc[(k + 1) * quarter:(k + 2) * quarter, :])

    def drain(p, carry):
        leave(p).wait()
        return carry

    lax.fori_loop(0, groups + UNROLL, drain, 0)


def item_kernel(*refs):
    head_ref, group_ref, spot_ref, block_ref, users_ref, weight_ref = refs[:6]
    piece_refs = refs[6:14]
    item_own, item_0, item_1, item_2, item_3 = refs[14:19]
    items_ref, item_acc, buf, sems, piece_sems = refs[19:]
    edge = buf.shape[2]
    rank = users_ref.shape[1]
    groups = head_ref[0, 2]

    loads = loads_of(piece_refs, items_ref, piece_sems)
    for c in loads:
        c.start()

    def fetch(p):
        slot = lax.rem(p, SLOTS)
        for k in range(GROUP):
            spot = spot_ref[0, GROUP * p + k]
            pltpu.make_async_copy(weight_ref.at[spot], buf.at[slot, k], sems.at[slot]).start()

    def arrive(p):
        slot = lax.rem(p, SLOTS)
        pltpu.make_async_copy(weight_ref.at[pl.ds(0, GROUP)], buf.at[slot], sems.at[slot]).wait()

    ahead = SLOTS - UNROLL
    for s in range(ahead):
        fetch(s)

    item_acc[...] = jnp.zeros(item_acc.shape, jnp.float32)
    user_gram = dot(users_ref[...], users_ref[...], 0, 0)
    high, low = split(GRAM_WEIGHT * user_gram)

    def visit(i, carry):
        base = i * UNROLL
        for j in range(UNROLL):
            arrive(base + j)
        for j in range(UNROLL):
            fetch(base + j + ahead)

        terms = []
        for j in range(UNROLL):
            g = base + j
            parts = []
            for k in range(GROUP):
                u = pl.multiple_of(block_ref[0, GROUP * g + k] * edge, edge)
                parts.append(users_ref[pl.ds(u, edge), :])
            weights = buf[lax.rem(g, SLOTS)].reshape(GROUP * edge, edge)
            terms.append(dot(weights, jnp.concatenate(parts, axis=0), 0, 0))
        for j in range(UNROLL):
            r = pl.multiple_of(group_ref[0, base + j] * edge, edge)
            item_acc[pl.ds(r, edge), :] += terms[j]
        return carry

    lax.fori_loop(0, groups // UNROLL, visit, 0)
    for j in range(ahead):
        arrive(groups + j)
    for c in loads:
        c.wait()
    part = item_0.shape[0] - TAIL
    for k, out in enumerate((None, None, None, None, item_0, item_1, item_2, item_3)):
        items = items_ref[RING * k:RING * (k + 1)].reshape(part, rank)
        total = item_acc[k * part:(k + 1) * part, :] + (dot(items, high, 1, 0) + dot(items, low, 1, 0))
        if out is None:
            item_own[k * part:(k + 1) * part, :] = total
        else:
            encode(out, total)


def user_sum_kernel(after_ref, own_ref, p1, p2, p3, out_ref):
    encode(out_ref, (own_ref[...] + decode(p1)) + (decode(p2) + decode(p3)))


def user_out_kernel(here_ref, p0, p1, p2, p3, out_ref):
    quarter = p0.shape[0] - TAIL
    for k, p in enumerate((p0, p1, p2, p3)):
        q = pl.multiple_of(((here_ref[1] - k) & 3) * quarter, quarter)
        out_ref[pl.ds(q, quarter), :] = GRAD_SCALE * decode(p)


def item_core_kernel(own_ref, c0, c1, c2, c3, own_out, p1, p2, p3):
    part = own_out.shape[0]
    own_out[...] = own_ref[:part, :] + decode(c0)
    for k, (c, out) in enumerate(((c1, p1), (c2, p2), (c3, p3))):
        encode(out, own_ref[(k + 1) * part:(k + 2) * part, :] + decode(c))


def item_mid_kernel(own_ref, c1, c2, c3, own_out, p1, p2, p3):
    part = own_out.shape[0]
    total = (own_ref[...] + decode(c1)) + (decode(c2) + decode(c3))
    own_out[...] = total[:part]
    for k, out in enumerate((p1, p2, p3)):
        encode(out, total[(k + 1) * part:(k + 2) * part])


def item_out_kernel(own_ref, p1, p2, p3, out_ref):
    out_ref[...] = GRAD_SCALE * ((own_ref[...] + decode(p1)) + (decode(p2) + decode(p3)))


def smem():
    return pl.BlockSpec(memory_space=pltpu.SMEM)


def vmem():
    return pl.BlockSpec(memory_space=pltpu.VMEM)


def anywhere():
    return pl.BlockSpec(memory_space=pl.ANY)


def f32(*shape):
    return jax.ShapeDtypeStruct(shape, jnp.float32)


def i32(*shape):
    return jax.ShapeDtypeStruct(shape, jnp.int32)


def bf16(*shape):
    return jax.ShapeDtypeStruct(shape, jnp.bfloat16)


def i16(*shape):
    return jax.ShapeDtypeStruct(shape, jnp.int16)


def local(user_factors, item_factors, confidence, tile_counts, tile_user, tile_item, block_slot, live_tiles):
    rows, rank = user_factors.shape
    tiles, edge = confidence.shape[2:4]
    blocks = rows // edge
    pairs = ((tiles + (GROUP - 1) * blocks) // GROUP + UNROLL - 1) // UNROLL * UNROLL + UNROLL
    users_size = lax.axis_size("users")
    items_size = lax.axis_size("items")
    spots = range(users_size)

    def along_y(a, k):
        return lax.ppermute(a, "items", [(i, (i + k) % items_size) for i in range(items_size)])

    def move(i, by_z, k):
        z, x, core = i // 8, i // 2 % 4, i % 2
        if by_z:
            z = (z + k) % 4
        else:
            x = (x + k) % 4
        return z * 8 + x * 2 + core

    def along_first(a, k):
        return lax.ppermute(a, "users", [(i, move(i, i % 2 == 0, k)) for i in spots])

    def along_second(a, k):
        return lax.ppermute(a, "users", [(i, move(i, i % 2 == 1, k)) for i in spots])

    def to_core(a):
        return lax.ppermute(a, "users", [(i, i ^ 1) for i in spots])

    where = lax.broadcasted_iota(jnp.int32, (2,), 0)
    here = jnp.where(where == 0, lax.axis_index("users"), lax.axis_index("items")).astype(jnp.int32)

    own = item_factors[0]
    first = [own] + [along_first(own, k) for k in (1, 2, 3)]
    spot_total = -(-(max(GROUP * pairs, tiles + (GROUP - 1) * users_size) + GROUP * (SLOTS + UNROLL)) // 128) * 128
    plan = pl.pallas_call(
        plan_kernel,
        out_shape=(i32(1, 128), i32(1, 128), i32(1, spot_total), i32(1, spot_total), f32(1, spot_total), i32(1, 128), i32(1, spot_total), i32(1, spot_total)),
        in_specs=[smem()] * 2 + [vmem()] * 4,
        out_specs=[vmem()] * 8,
        name="plan",
    )(here, live_tiles[0], tile_user[0], tile_item[0], tile_counts[0], block_slot)
    first = jnp.stack(first)
    first, plan = lax.optimization_barrier((first, plan))
    pieces = [first] + [along_second(first, k) for k in (1, 2, 3)]
    pieces += [to_core(a) for a in pieces]

    quarter = rows // 4
    panels = users_size
    half_rows = panels * edge // 2
    part = half_rows // 4
    head, pair, tile, panel, factor, group, spot, block = plan
    *user_parts, weights = pl.pallas_call(
        user_kernel,
        out_shape=(f32(quarter, rank),) + (i16(quarter + TAIL, rank),) * 3 + (bf16(GROUP * pairs, edge, edge),),
        in_specs=[smem()] * 5 + [vmem(), anywhere()] + [anywhere()] * 8,
        out_specs=[vmem()] * 4 + [anywhere()],
        scratch_shapes=[
            pltpu.VMEM((panels, edge, rank), jnp.bfloat16),
            pltpu.VMEM((rows, rank), jnp.float32),
            pltpu.VMEM((SLOTS, GROUP, edge, edge), jnp.bfloat16),
            pltpu.VMEM((GROUP * pairs, edge, edge), jnp.bfloat16),
            pltpu.SemaphoreType.DMA((SLOTS,)),
            pltpu.SemaphoreType.DMA((8,)),
            pltpu.SemaphoreType.DMA((pairs,)),
        ],
        name="tiles_user",
    )(head, pair, tile, panel, factor, user_factors, confidence[0, 0], *pieces)
    item_own, *item_parts = pl.pallas_call(
        item_kernel,
        out_shape=(f32(half_rows, rank),) + (i16(part + TAIL, rank),) * 4,
        in_specs=[smem()] * 4 + [vmem(), anywhere()] + [anywhere()] * 8,
        out_specs=[vmem()] * 5,
        scratch_shapes=[
            pltpu.VMEM((panels, edge, rank), jnp.bfloat16),
            pltpu.VMEM((panels * edge, rank), jnp.float32),
            pltpu.VMEM((SLOTS, GROUP, edge, edge), jnp.bfloat16),
            pltpu.SemaphoreType.DMA((SLOTS,)),
            pltpu.SemaphoreType.DMA((8,)),
        ],
        name="tiles_item",
    )(head, group, spot, block, user_factors, weights, *pieces)
    user_own, *user_parts = user_parts
    after = item_own

    item_parts = [to_core(a) for a in item_parts]
    user_parts = [along_y(a, -k) for k, a in zip((1, 2, 3), user_parts)]

    user_code = pl.pallas_call(
        user_sum_kernel,
        out_shape=i16(quarter + TAIL, rank),
        in_specs=[anywhere()] + [vmem()] * 4,
        out_specs=vmem(),
        name="user_sum",
    )(after, user_own, *user_parts)
    def item_stage(kernel, name, size, *ins):
        return pl.pallas_call(
            kernel,
            out_shape=(f32(size, rank),) + (i16(size + TAIL, rank),) * 3,
            in_specs=[vmem()] * len(ins),
            out_specs=[vmem()] * 4,
            name=name,
        )(*ins)

    item_own, *item_parts = item_stage(item_core_kernel, "item_core", part, item_own, *item_parts)
    item_parts = [along_second(a, -k) for k, a in zip((1, 2, 3), item_parts)]
    user_codes = [user_code] + [along_y(user_code, k) for k in (1, 2, 3)]
    item_own, *item_parts = item_stage(item_mid_kernel, "item_mid", edge, item_own, *item_parts)
    item_parts = [along_first(a, -k) for k, a in zip((1, 2, 3), item_parts)]
    item_grad = pl.pallas_call(
        item_out_kernel,
        out_shape=f32(edge, rank),
        in_specs=[vmem()] * 4,
        out_specs=vmem(),
        name="item_out",
    )(item_own, *item_parts)
    user_grad = pl.pallas_call(
        user_out_kernel,
        out_shape=f32(rows, rank),
        in_specs=[smem()] + [vmem()] * 4,
        out_specs=vmem(),
        name="user_out",
    )(here, *user_codes)
    return user_grad, item_grad[None]


def solution(mesh):
    in_specs = (
        P("users", None),
        P("items", "users", None),
        P("users", "items", None, None, None),
        P("users", "items", None),
        P("users", "items", None),
        P("users", "items", None),
        P("items", None),
        P("users", "items"),
    )
    out_specs = (P("users", None), P("items", "users", None))
    return jax.shard_map(local, mesh=mesh, in_specs=in_specs, out_specs=out_specs, check_vma=False)
```

```python
import jax
import jax.numpy as jnp
from jax import lax
from jax.experimental import pallas as pl
from jax.experimental.pallas import tpu as pltpu
from jax.sharding import PartitionSpec as P


GRAD_SCALE = 0.005
GRAM_WEIGHT = 0.5
SLOTS = 8
GROUP = 4
UNROLL = 2
RING = 4
TAIL = 16
TOP = 32000.0


def dot(a, b, ca, cb):
    return lax.dot_general(a, b, (((ca,), (cb,)), ((), ())), preferred_element_type=jnp.float32)


def split(x):
    high = x.astype(jnp.bfloat16)
    return high, (x - high.astype(jnp.float32)).astype(jnp.bfloat16)


def encode(out_ref, x):
    rows = x.shape[0]
    top = jnp.max(jnp.abs(x), axis=0, keepdims=True)
    power = jnp.ceil(jnp.log2(jnp.maximum(top, 1e-30) * (1.0 / TOP)))
    out_ref[:rows, :] = jnp.round(x * jnp.exp2(-power)).astype(jnp.int32).astype(jnp.int16)
    tail = jnp.broadcast_to(power, (TAIL, x.shape[1]))
    out_ref[rows:, :] = tail.astype(jnp.int32).astype(jnp.int16)


def decode(ref):
    rows = ref.shape[0] - TAIL
    power = ref[rows:, :].astype(jnp.int32).astype(jnp.float32)[:1]
    return ref[:rows, :].astype(jnp.int32).astype(jnp.float32) * jnp.exp2(power)


def plan_kernel(here_ref, live_ref, user_ref, item_ref, count_ref, slot_ref, head_ref, pair_ref, tile_ref, panel_ref, factor_ref, group_ref, weight_ref, block_ref):
    tiles = user_ref.shape[1]
    spots = tile_ref.shape[1]
    panels = slot_ref.shape[1]
    z = here_ref[0] // 8
    x = (here_ref[0] // 2) & 3
    core = here_ref[0] & 1

    def grid(rows, lanes, axis):
        return lax.broadcasted_iota(jnp.int32, (rows, lanes), axis)

    down = grid(tiles, tiles, 0)
    across = grid(tiles, tiles, 1)

    def pick(mask, values, axis):
        return jnp.sum(jnp.where(mask, values, 0.0), axis=axis, keepdims=True)

    def column(row):
        return pick(down == across, row.astype(jnp.float32), 1)

    user_row = user_ref[...]
    user = column(user_row)
    user_int = user.astype(jnp.int32)
    order = grid(tiles, 1, 0)
    used = order < live_ref[0]
    rank = pick((user_int == user_row) & (across < down), jnp.ones((1, 1), jnp.float32), 1)
    own = (user_int == grid(tiles, 128, 1)) & used
    sizes = pick(own, jnp.ones((1, 1), jnp.float32), 0).astype(jnp.int32)
    groups = ((sizes + (GROUP - 1)) // GROUP).astype(jnp.float32)
    first = pick(grid(tiles, 128, 1) < user_int, groups, 1)
    spot = jnp.where(used, GROUP * first + rank, -1.0).astype(jnp.int32)
    item = column(item_ref[...]).astype(jnp.int32)
    slot = pick(item == grid(tiles, panels, 1), slot_ref[...].astype(jnp.float32), 1).astype(jnp.int32)
    far_z = (z - (slot >> 3)) & 3
    far_x = (x - (slot >> 1)) & 3
    odd = (slot & 1) == 1
    panel = ((core + slot) & 1) * 16 + jnp.where(odd, far_z * 4 + far_x, far_x * 4 + far_z)
    factor = jnp.log(1.0 + column(count_ref[...]))
    at = spot == grid(tiles, spots, 1)
    tile_ref[...] = pick(at, order.astype(jnp.float32), 0).astype(jnp.int32)
    panel_ref[...] = pick(at, panel.astype(jnp.float32), 0).astype(jnp.int32)
    factor_ref[...] = pick(at, factor, 0)
    pair_ref[...] = pick(spot == GROUP * grid(tiles, pair_ref.shape[1], 1), user, 0).astype(jnp.int32)
    total = jnp.sum(groups, axis=1, keepdims=True)
    empty = GROUP * total
    panel_row = pick(down == across, panel.astype(jnp.float32), 0).astype(jnp.int32)
    rank = pick((panel == panel_row) & (across < down), jnp.ones((1, 1), jnp.float32), 1)
    own = (panel == grid(tiles, 128, 1)) & used
    sizes = pick(own, jnp.ones((1, 1), jnp.float32), 0).astype(jnp.int32)
    groups = ((sizes + (GROUP - 1)) // GROUP).astype(jnp.float32)
    first = pick(grid(tiles, 128, 1) < panel, groups, 1)
    place = jnp.where(used, GROUP * first + rank, -1.0).astype(jnp.int32)
    at = place == grid(tiles, spots, 1)
    weight_ref[...] = (pick(at, spot.astype(jnp.float32) - empty, 0) + empty).astype(jnp.int32)
    block_ref[...] = pick(at, user, 0).astype(jnp.int32)
    group_ref[...] = pick(place == GROUP * grid(tiles, 128, 1), panel.astype(jnp.float32), 0).astype(jnp.int32)
    lane = grid(1, 128, 1)
    item_total = jnp.sum(groups, axis=1, keepdims=True)
    numbers = jnp.where(lane == 0, total, item_total).astype(jnp.int32)
    rounded = (numbers + (UNROLL - 1)) // UNROLL * UNROLL
    head_ref[...] = jnp.where(lane == 1, here_ref[1], rounded)


def loads_of(piece_refs, items_ref, sems):
    return [
        pltpu.make_async_copy(piece, items_ref.at[pl.ds(RING * i, RING)], sems.at[i])
        for i, piece in enumerate(piece_refs)
    ]


def user_kernel(*refs):
    head_ref, pair_ref, tile_ref, panel_ref, factor_ref, users_ref, conf_ref = refs[:7]
    piece_refs = refs[7:15]
    user_own, user_1, user_2, user_3, weight_out = refs[15:20]
    items_ref, user_acc, conf_buf, weights_ref, sems, piece_sems, out_sems = refs[20:]
    edge = conf_buf.shape[2]
    rank = users_ref.shape[1]
    groups = head_ref[0, 0]
    y = head_ref[0, 1]

    loads = loads_of(piece_refs, items_ref, piece_sems)
    for c in loads:
        c.start()

    def fetch(p):
        slot = lax.rem(p, SLOTS)
        for k in range(GROUP):
            tile = tile_ref[0, GROUP * p + k]
            pltpu.make_async_copy(conf_ref.at[tile], conf_buf.at[slot, k], sems.at[slot]).start()

    def arrive(p):
        slot = lax.rem(p, SLOTS)
        pltpu.make_async_copy(conf_ref.at[pl.ds(0, GROUP)], conf_buf.at[slot], sems.at[slot]).wait()

    def leave(p):
        rows = pl.ds(GROUP * p, GROUP)
        return pltpu.make_async_copy(weights_ref.at[rows], weight_out.at[rows], out_sems.at[p])

    for s in range(SLOTS):
        fetch(s)

    item_gram = jnp.zeros((rank, rank), jnp.float32)
    for i, c in enumerate(loads):
        c.wait()
        rows = items_ref[RING * i:RING * (i + 1)].reshape(-1, rank)
        item_gram = item_gram + dot(rows, rows, 0, 0)
    high, low = split(GRAM_WEIGHT * item_gram)
    quarter = user_acc.shape[0] // RING
    for k in range(RING):
        q = pl.multiple_of(((y - k) & 3) * quarter, quarter)
        rows = users_ref[pl.ds(q, quarter), :]
        user_acc[k * quarter:(k + 1) * quarter, :] = dot(rows, high, 1, 0) + dot(rows, low, 1, 0)

    def prepare(g):
        slot = lax.rem(g, SLOTS)
        u = pl.multiple_of(pair_ref[0, g] * edge, edge)
        users = users_ref[pl.ds(u, edge), :]
        scores = []
        for j in range(GROUP // 2):
            v0 = panel_ref[0, GROUP * g + 2 * j]
            v1 = panel_ref[0, GROUP * g + 2 * j + 1]
            items = jnp.concatenate([items_ref[v0], items_ref[v1]], axis=0)
            scores.append(dot(users, items, 1, 1))
        for k in range(GROUP):
            part = scores[k // 2][:, (k % 2) * edge:(k % 2 + 1) * edge]
            weight = conf_buf[slot, k].astype(jnp.float32) * factor_ref[0, GROUP * g + k] * (part - 1.0)
            weights_ref[GROUP * g + k] = weight.astype(jnp.bfloat16)

    for j in range(UNROLL):
        arrive(j)
    for j in range(UNROLL):
        prepare(j)

    def visit(i, carry):
        base = i * UNROLL
        for j in range(UNROLL):
            arrive(base + UNROLL + j)
        for j in range(UNROLL):
            fetch(base + j + SLOTS)
            leave(base + j).start()
        terms = []
        for j in range(UNROLL):
            g = base + j
            items = jnp.concatenate([items_ref[panel_ref[0, GROUP * g + k]] for k in range(GROUP)], axis=0)
            weights = jnp.concatenate([weights_ref[GROUP * g + k] for k in range(GROUP)], axis=1)
            terms.append(dot(weights, items, 1, 0))
        for j in range(UNROLL):
            prepare(base + UNROLL + j)
        for j in range(UNROLL):
            b = pair_ref[0, base + j]
            r = pl.multiple_of(((((y - (b >> 2)) & 3) << 2) + (b & 3)) * edge, edge)
            user_acc[pl.ds(r, edge), :] += terms[j]
        return carry

    lax.fori_loop(0, groups // UNROLL, visit, 0)
    for j in range(UNROLL):
        leave(groups + j).start()
    for j in range(UNROLL, SLOTS):
        arrive(groups + j)
    user_own[...] = user_acc[:quarter, :]
    for k, out in enumerate((user_1, user_2, user_3)):
        encode(out, user_acc[(k + 1) * quarter:(k + 2) * quarter, :])

    def drain(p, carry):
        leave(p).wait()
        return carry

    lax.fori_loop(0, groups + UNROLL, drain, 0)


def item_kernel(*refs):
    head_ref, group_ref, spot_ref, block_ref, users_ref, weight_ref = refs[:6]
    piece_refs = refs[6:14]
    item_own, item_0, item_1, item_2, item_3 = refs[14:19]
    items_ref, item_acc, buf, sems, piece_sems = refs[19:]
    edge = buf.shape[2]
    rank = users_ref.shape[1]
    groups = head_ref[0, 2]

    loads = loads_of(piece_refs, items_ref, piece_sems)
    for c in loads:
        c.start()

    def fetch(p):
        slot = lax.rem(p, SLOTS)
        for k in range(GROUP):
            spot = spot_ref[0, GROUP * p + k]
            pltpu.make_async_copy(weight_ref.at[spot], buf.at[slot, k], sems.at[slot]).start()

    def arrive(p):
        slot = lax.rem(p, SLOTS)
        pltpu.make_async_copy(weight_ref.at[pl.ds(0, GROUP)], buf.at[slot], sems.at[slot]).wait()

    ahead = SLOTS - UNROLL
    for s in range(ahead):
        fetch(s)

    item_acc[...] = jnp.zeros(item_acc.shape, jnp.float32)
    user_gram = dot(users_ref[...], users_ref[...], 0, 0)
    high, low = split(GRAM_WEIGHT * user_gram)

    def visit(i, carry):
        base = i * UNROLL
        for j in range(UNROLL):
            arrive(base + j)
        for j in range(UNROLL):
            fetch(base + j + ahead)

        terms = []
        for j in range(UNROLL):
            g = base + j
            parts = []
            for k in range(GROUP):
                u = pl.multiple_of(block_ref[0, GROUP * g + k] * edge, edge)
                parts.append(users_ref[pl.ds(u, edge), :])
            weights = buf[lax.rem(g, SLOTS)].reshape(GROUP * edge, edge)
            terms.append(dot(weights, jnp.concatenate(parts, axis=0), 0, 0))
        for j in range(UNROLL):
            r = pl.multiple_of(group_ref[0, base + j] * edge, edge)
            item_acc[pl.ds(r, edge), :] += terms[j]
        return carry

    lax.fori_loop(0, groups // UNROLL, visit, 0)
    for j in range(ahead):
        arrive(groups + j)
    for c in loads:
        c.wait()
    part = item_0.shape[0] - TAIL
    for k, out in enumerate((None, None, None, None, item_0, item_1, item_2, item_3)):
        items = items_ref[RING * k:RING * (k + 1)].reshape(part, rank)
        total = item_acc[k * part:(k + 1) * part, :] + (dot(items, high, 1, 0) + dot(items, low, 1, 0))
        if out is None:
            item_own[k * part:(k + 1) * part, :] = total
        else:
            encode(out, total)


def user_sum_kernel(after_ref, own_ref, p1, p2, p3, out_ref):
    encode(out_ref, (own_ref[...] + decode(p1)) + (decode(p2) + decode(p3)))


def user_out_kernel(here_ref, p0, p1, p2, p3, out_ref):
    quarter = p0.shape[0] - TAIL
    for k, p in enumerate((p0, p1, p2, p3)):
        q = pl.multiple_of(((here_ref[1] - k) & 3) * quarter, quarter)
        out_ref[pl.ds(q, quarter), :] = GRAD_SCALE * decode(p)


def item_core_kernel(own_ref, c0, c1, c2, c3, own_out, p1, p2, p3):
    part = own_out.shape[0]
    own_out[...] = own_ref[:part, :] + decode(c0)
    for k, (c, out) in enumerate(((c1, p1), (c2, p2), (c3, p3))):
        encode(out, own_ref[(k + 1) * part:(k + 2) * part, :] + decode(c))


def item_mid_kernel(own_ref, c1, c2, c3, own_out, p1, p2, p3):
    part = own_out.shape[0]
    total = (own_ref[...] + decode(c1)) + (decode(c2) + decode(c3))
    own_out[...] = total[:part]
    for k, out in enumerate((p1, p2, p3)):
        encode(out, total[(k + 1) * part:(k + 2) * part])


def item_out_kernel(own_ref, p1, p2, p3, out_ref):
    out_ref[...] = GRAD_SCALE * ((own_ref[...] + decode(p1)) + (decode(p2) + decode(p3)))


def smem():
    return pl.BlockSpec(memory_space=pltpu.SMEM)


def vmem():
    return pl.BlockSpec(memory_space=pltpu.VMEM)


def anywhere():
    return pl.BlockSpec(memory_space=pl.ANY)


def f32(*shape):
    return jax.ShapeDtypeStruct(shape, jnp.float32)


def i32(*shape):
    return jax.ShapeDtypeStruct(shape, jnp.int32)


def bf16(*shape):
    return jax.ShapeDtypeStruct(shape, jnp.bfloat16)


def i16(*shape):
    return jax.ShapeDtypeStruct(shape, jnp.int16)


def local(user_factors, item_factors, confidence, tile_counts, tile_user, tile_item, block_slot, live_tiles):
    rows, rank = user_factors.shape
    tiles, edge = confidence.shape[2:4]
    blocks = rows // edge
    pairs = ((tiles + (GROUP - 1) * blocks) // GROUP + UNROLL - 1) // UNROLL * UNROLL + UNROLL
    users_size = lax.axis_size("users")
    items_size = lax.axis_size("items")
    spots = range(users_size)

    def along_y(a, k):
        return lax.ppermute(a, "items", [(i, (i + k) % items_size) for i in range(items_size)])

    def move(i, by_z, k):
        z, x, core = i // 8, i // 2 % 4, i % 2
        if by_z:
            z = (z + k) % 4
        else:
            x = (x + k) % 4
        return z * 8 + x * 2 + core

    def along_first(a, k):
        return lax.ppermute(a, "users", [(i, move(i, i % 2 == 0, k)) for i in spots])

    def along_second(a, k):
        return lax.ppermute(a, "users", [(i, move(i, i % 2 == 1, k)) for i in spots])

    def to_core(a):
        return lax.ppermute(a, "users", [(i, i ^ 1) for i in spots])

    where = lax.broadcasted_iota(jnp.int32, (2,), 0)
    here = jnp.where(where == 0, lax.axis_index("users"), lax.axis_index("items")).astype(jnp.int32)

    own = item_factors[0]
    first = [own] + [along_first(own, k) for k in (1, 2, 3)]
    spot_total = -(-(max(GROUP * pairs, tiles + (GROUP - 1) * users_size) + GROUP * (SLOTS + UNROLL)) // 128) * 128
    plan = pl.pallas_call(
        plan_kernel,
        out_shape=(i32(1, 128), i32(1, 128), i32(1, spot_total), i32(1, spot_total), f32(1, spot_total), i32(1, 128), i32(1, spot_total), i32(1, spot_total)),
        in_specs=[smem()] * 2 + [vmem()] * 4,
        out_specs=[vmem()] * 8,
        name="plan",
    )(here, live_tiles[0], tile_user[0], tile_item[0], tile_counts[0], block_slot)
    first = jnp.stack(first)
    first, plan = lax.optimization_barrier((first, plan))
    pieces = [first] + [along_second(first, k) for k in (1, 2, 3)]
    pieces += [to_core(a) for a in pieces]

    quarter = rows // 4
    panels = users_size
    half_rows = panels * edge // 2
    part = half_rows // 4
    head, pair, tile, panel, factor, group, spot, block = plan
    *user_parts, weights = pl.pallas_call(
        user_kernel,
        out_shape=(f32(quarter, rank),) + (i16(quarter + TAIL, rank),) * 3 + (bf16(GROUP * pairs, edge, edge),),
        in_specs=[smem()] * 5 + [vmem(), anywhere()] + [anywhere()] * 8,
        out_specs=[vmem()] * 4 + [anywhere()],
        scratch_shapes=[
            pltpu.VMEM((panels, edge, rank), jnp.bfloat16),
            pltpu.VMEM((rows, rank), jnp.float32),
            pltpu.VMEM((SLOTS, GROUP, edge, edge), jnp.bfloat16),
            pltpu.VMEM((GROUP * pairs, edge, edge), jnp.bfloat16),
            pltpu.SemaphoreType.DMA((SLOTS,)),
            pltpu.SemaphoreType.DMA((8,)),
            pltpu.SemaphoreType.DMA((pairs,)),
        ],
        name="tiles_user",
    )(head, pair, tile, panel, factor, user_factors, confidence[0, 0], *pieces)
    item_own, *item_parts = pl.pallas_call(
        item_kernel,
        out_shape=(f32(half_rows, rank),) + (i16(part + TAIL, rank),) * 4,
        in_specs=[smem()] * 4 + [vmem(), anywhere()] + [anywhere()] * 8,
        out_specs=[vmem()] * 5,
        scratch_shapes=[
            pltpu.VMEM((panels, edge, rank), jnp.bfloat16),
            pltpu.VMEM((panels * edge, rank), jnp.float32),
            pltpu.VMEM((SLOTS, GROUP, edge, edge), jnp.bfloat16),
            pltpu.SemaphoreType.DMA((SLOTS,)),
            pltpu.SemaphoreType.DMA((8,)),
        ],
        name="tiles_item",
    )(head, group, spot, block, user_factors, weights, *pieces)
    user_own, *user_parts = user_parts
    after = item_own

    item_parts = [to_core(a) for a in item_parts]
    user_parts = [along_y(a, -k) for k, a in zip((1, 2, 3), user_parts)]

    user_code = pl.pallas_call(
        user_sum_kernel,
        out_shape=i16(quarter + TAIL, rank),
        in_specs=[anywhere()] + [vmem()] * 4,
        out_specs=vmem(),
        name="user_sum",
    )(after, user_own, *user_parts)

    def item_stage(kernel, size, *ins):
        return pl.pallas_call(
            kernel,
            out_shape=(f32(size, rank),) + (i16(size + TAIL, rank),) * 3,
            in_specs=[vmem()] * len(ins),
            out_specs=[vmem()] * 4,
        )(*ins)

    item_own, *item_parts = item_stage(item_core_kernel, part, item_own, *item_parts)
    item_parts = [along_second(a, -k) for k, a in zip((1, 2, 3), item_parts)]
    user_codes = [user_code] + [along_y(user_code, k) for k in (1, 2, 3)]
    item_own, *item_parts = item_stage(item_mid_kernel, edge, item_own, *item_parts)
    item_parts = [along_first(a, -k) for k, a in zip((1, 2, 3), item_parts)]
    item_grad = pl.pallas_call(
        item_out_kernel,
        out_shape=f32(edge, rank),
        in_specs=[vmem()] * 4,
        out_specs=vmem(),
        name="item_out",
    )(item_own, *item_parts)
    user_grad = pl.pallas_call(
        user_out_kernel,
        out_shape=f32(rows, rank),
        in_specs=[smem()] + [vmem()] * 4,
        out_specs=vmem(),
        name="user_out",
    )(here, *user_codes)
    return user_grad, item_grad[None]


def solution(mesh):
    in_specs = (
        P("users", None),
        P("items", "users", None),
        P("users", "items", None, None, None),
        P("users", "items", None),
        P("users", "items", None),
        P("users", "items", None),
        P("items", None),
        P("users", "items"),
    )
    out_specs = (P("users", None), P("items", "users", None))

    return jax.shard_map(local, mesh=mesh, in_specs=in_specs, out_specs=out_specs, check_vma=False)
```

```python
import jax
import jax.numpy as jnp
from jax import lax
from jax.experimental import pallas as pl
from jax.experimental.pallas import tpu as pltpu
from jax.sharding import PartitionSpec as P


GRAD_SCALE = 0.005
GRAM_WEIGHT = 0.5
SLOTS = 8
GROUP = 4
UNROLL = 2
TURNS = 8
RING = 4
TAIL = 16
TOP = 32000.0


def dot(a, b, ca, cb):
    return lax.dot_general(a, b, (((ca,), (cb,)), ((), ())), preferred_element_type=jnp.float32)


def split(x):
    high = x.astype(jnp.bfloat16)
    return high, (x - high.astype(jnp.float32)).astype(jnp.bfloat16)


def encode(out_ref, x):
    rows = x.shape[0]
    top = jnp.max(jnp.abs(x), axis=0, keepdims=True)
    power = jnp.ceil(jnp.log2(jnp.maximum(top, 1e-30) * (1.0 / TOP)))
    out_ref[:rows, :] = jnp.round(x * jnp.exp2(-power)).astype(jnp.int32).astype(jnp.int16)
    tail = jnp.broadcast_to(power, (TAIL, x.shape[1]))
    out_ref[rows:, :] = tail.astype(jnp.int32).astype(jnp.int16)


def decode(ref):
    rows = ref.shape[0] - TAIL
    power = ref[rows:, :].astype(jnp.int32).astype(jnp.float32)[:1]
    return ref[:rows, :].astype(jnp.int32).astype(jnp.float32) * jnp.exp2(power)


def plan_kernel(here_ref, live_ref, user_ref, item_ref, count_ref, slot_ref, head_ref, pair_ref, tile_ref, panel_ref, factor_ref, group_ref, weight_ref, block_ref):
    tiles = user_ref.shape[1]
    spots = tile_ref.shape[1]
    panels = slot_ref.shape[1]
    z = here_ref[0] // 8
    x = (here_ref[0] // 2) & 3
    core = here_ref[0] & 1

    def grid(rows, lanes, axis):
        return lax.broadcasted_iota(jnp.int32, (rows, lanes), axis)

    down = grid(tiles, tiles, 0)
    across = grid(tiles, tiles, 1)

    def pick(mask, values, axis):
        return jnp.sum(jnp.where(mask, values, 0.0), axis=axis, keepdims=True)

    def column(row):
        return pick(down == across, row.astype(jnp.float32), 1)

    user_row = user_ref[...]
    user = column(user_row)
    user_int = user.astype(jnp.int32)
    order = grid(tiles, 1, 0)
    used = order < live_ref[0]
    rank = pick((user_int == user_row) & (across < down), jnp.ones((1, 1), jnp.float32), 1)
    own = (user_int == grid(tiles, 128, 1)) & used
    sizes = pick(own, jnp.ones((1, 1), jnp.float32), 0).astype(jnp.int32)
    groups = ((sizes + (GROUP - 1)) // GROUP).astype(jnp.float32)
    first = pick(grid(tiles, 128, 1) < user_int, groups, 1)
    spot = jnp.where(used, GROUP * first + rank, -1.0).astype(jnp.int32)
    item = column(item_ref[...]).astype(jnp.int32)
    slot = pick(item == grid(tiles, panels, 1), slot_ref[...].astype(jnp.float32), 1).astype(jnp.int32)
    far_z = (z - (slot >> 3)) & 3
    far_x = (x - (slot >> 1)) & 3
    odd = (slot & 1) == 1
    panel = ((core + slot) & 1) * 16 + jnp.where(odd, far_z * 4 + far_x, far_x * 4 + far_z)
    factor = jnp.log(1.0 + column(count_ref[...]))
    at = spot == grid(tiles, spots, 1)
    tile_ref[...] = pick(at, order.astype(jnp.float32), 0).astype(jnp.int32)
    panel_ref[...] = pick(at, panel.astype(jnp.float32), 0).astype(jnp.int32)
    factor_ref[...] = pick(at, factor, 0)
    pair_ref[...] = pick(spot == GROUP * grid(tiles, pair_ref.shape[1], 1), user, 0).astype(jnp.int32)
    total = jnp.sum(groups, axis=1, keepdims=True)
    empty = GROUP * total
    panel_row = pick(down == across, panel.astype(jnp.float32), 0).astype(jnp.int32)
    rank = pick((panel == panel_row) & (across < down), jnp.ones((1, 1), jnp.float32), 1)
    own = (panel == grid(tiles, 128, 1)) & used
    sizes = pick(own, jnp.ones((1, 1), jnp.float32), 0).astype(jnp.int32)
    groups = ((sizes + (GROUP - 1)) // GROUP).astype(jnp.float32)
    first = pick(grid(tiles, 128, 1) < panel, groups, 1)
    place = jnp.where(used, GROUP * first + rank, -1.0).astype(jnp.int32)
    at = place == grid(tiles, spots, 1)
    weight_ref[...] = (pick(at, spot.astype(jnp.float32) - empty, 0) + empty).astype(jnp.int32)
    block_ref[...] = pick(at, user, 0).astype(jnp.int32)
    group_ref[...] = pick(place == GROUP * grid(tiles, 128, 1), panel.astype(jnp.float32), 0).astype(jnp.int32)
    lane = grid(1, 128, 1)
    item_total = jnp.sum(groups, axis=1, keepdims=True)
    numbers = jnp.where(lane == 0, total, item_total).astype(jnp.int32)
    users_rounded = (numbers + (UNROLL - 1)) // UNROLL * UNROLL
    items_rounded = (numbers + (TURNS - 1)) // TURNS * TURNS
    head_ref[...] = jnp.where(lane == 1, here_ref[1], jnp.where(lane == 0, users_rounded, items_rounded))


def loads_of(piece_refs, items_ref, sems):
    return [
        pltpu.make_async_copy(piece, items_ref.at[pl.ds(RING * i, RING)], sems.at[i])
        for i, piece in enumerate(piece_refs)
    ]


def tile_kernel(*refs):
    head_ref, pair_ref, tile_ref, panel_ref, factor_ref, group_ref, spot_ref, block_ref, users_ref, conf_ref = refs[:10]
    piece_refs = refs[10:18]
    user_own, user_1, user_2, user_3, item_own, item_code = refs[18:24]
    items_ref, user_acc, item_acc, conf_buf, weights_ref, sems, piece_sems = refs[24:]
    edge = conf_buf.shape[2]
    rank = users_ref.shape[1]
    groups = head_ref[0, 0]
    y = head_ref[0, 1]

    loads = loads_of(piece_refs, items_ref, piece_sems)
    for c in loads:
        c.start()

    def fetch(p):
        slot = lax.rem(p, SLOTS)
        for k in range(GROUP):
            tile = tile_ref[0, GROUP * p + k]
            pltpu.make_async_copy(conf_ref.at[tile], conf_buf.at[slot, k], sems.at[slot]).start()

    def arrive(p):
        slot = lax.rem(p, SLOTS)
        pltpu.make_async_copy(conf_ref.at[pl.ds(0, GROUP)], conf_buf.at[slot], sems.at[slot]).wait()

    for s in range(SLOTS):
        fetch(s)

    user_gram = dot(users_ref[...], users_ref[...], 0, 0)
    user_high, user_low = split(GRAM_WEIGHT * user_gram)
    item_acc[...] = jnp.zeros(item_acc.shape, jnp.float32)
    item_gram = jnp.zeros((rank, rank), jnp.float32)
    for i, c in enumerate(loads):
        c.wait()
        rows = items_ref[RING * i:RING * (i + 1)].reshape(-1, rank)
        item_gram = item_gram + dot(rows, rows, 0, 0)
    high, low = split(GRAM_WEIGHT * item_gram)
    quarter = user_acc.shape[0] // RING
    for k in range(RING):
        q = pl.multiple_of(((y - k) & 3) * quarter, quarter)
        rows = users_ref[pl.ds(q, quarter), :]
        user_acc[k * quarter:(k + 1) * quarter, :] = dot(rows, high, 1, 0) + dot(rows, low, 1, 0)

    def prepare(g):
        slot = lax.rem(g, SLOTS)
        u = pl.multiple_of(pair_ref[0, g] * edge, edge)
        users = users_ref[pl.ds(u, edge), :]
        scores = []
        for j in range(GROUP // 2):
            v0 = panel_ref[0, GROUP * g + 2 * j]
            v1 = panel_ref[0, GROUP * g + 2 * j + 1]
            items = jnp.concatenate([items_ref[v0], items_ref[v1]], axis=0)
            scores.append(dot(users, items, 1, 1))
        for k in range(GROUP):
            part = scores[k // 2][:, (k % 2) * edge:(k % 2 + 1) * edge]
            weight = conf_buf[slot, k].astype(jnp.float32) * factor_ref[0, GROUP * g + k] * (part - 1.0)
            weights_ref[GROUP * g + k] = weight.astype(jnp.bfloat16)

    for j in range(UNROLL):
        arrive(j)
    for j in range(UNROLL):
        prepare(j)

    def visit(i, carry):
        base = i * UNROLL
        for j in range(UNROLL):
            arrive(base + UNROLL + j)
        for j in range(UNROLL):
            fetch(base + j + SLOTS)
        terms = []
        for j in range(UNROLL):
            g = base + j
            items = jnp.concatenate([items_ref[panel_ref[0, GROUP * g + k]] for k in range(GROUP)], axis=0)
            weights = jnp.concatenate([weights_ref[GROUP * g + k] for k in range(GROUP)], axis=1)
            terms.append(dot(weights, items, 1, 0))
        for j in range(UNROLL):
            prepare(base + UNROLL + j)
        for j in range(UNROLL):
            b = pair_ref[0, base + j]
            r = pl.multiple_of(((((y - (b >> 2)) & 3) << 2) + (b & 3)) * edge, edge)
            user_acc[pl.ds(r, edge), :] += terms[j]
        return carry

    lax.fori_loop(0, groups // UNROLL, visit, 0)
    for j in range(UNROLL, SLOTS):
        arrive(groups + j)

    def turn(i, carry):
        base = i * TURNS
        terms = []
        for j in range(TURNS):
            g = base + j
            parts = []
            for k in range(GROUP):
                u = pl.multiple_of(block_ref[0, GROUP * g + k] * edge, edge)
                parts.append(users_ref[pl.ds(u, edge), :])
            weights = jnp.concatenate([weights_ref[spot_ref[0, GROUP * g + k]] for k in range(GROUP)], axis=0)
            terms.append(dot(weights, jnp.concatenate(parts, axis=0), 0, 0))
        for j in range(TURNS):
            r = pl.multiple_of(group_ref[0, base + j] * edge, edge)
            item_acc[pl.ds(r, edge), :] += terms[j]
        return carry

    lax.fori_loop(0, head_ref[0, 2] // TURNS, turn, 0)
    user_own[...] = user_acc[:quarter, :]
    for k, out in enumerate((user_1, user_2, user_3)):
        encode(out, user_acc[(k + 1) * quarter:(k + 2) * quarter, :])
    part = item_acc.shape[0] // 8
    for k in range(8):
        items = items_ref[RING * k:RING * (k + 1)].reshape(part, rank)
        total = item_acc[k * part:(k + 1) * part, :] + (dot(items, user_high, 1, 0) + dot(items, user_low, 1, 0))
        if k < RING:
            item_own[k * part:(k + 1) * part, :] = total
        else:
            encode(item_code.at[pl.ds((k - RING) * (part + TAIL), part + TAIL)], total)


def user_sum_kernel(own_ref, p1, p2, p3, out_ref):
    encode(out_ref, (own_ref[...] + decode(p1)) + (decode(p2) + decode(p3)))


def final_kernel(here_ref, p0, p1, p2, p3, own_ref, q1, q2, q3, user_out, item_out, buf, sems):
    quarter = p0.shape[0] - TAIL
    copies = []
    for k, p in enumerate((p0, p1, p2, p3)):
        buf[k] = GRAD_SCALE * decode(p)
        q = pl.multiple_of(((here_ref[1] - k) & 3) * quarter, quarter)
        copies.append(pltpu.make_async_copy(buf.at[k], user_out.at[pl.ds(q, quarter)], sems.at[k]))
        copies[-1].start()
    item_out[...] = GRAD_SCALE * ((own_ref[...] + decode(q1)) + (decode(q2) + decode(q3)))
    for c in copies:
        c.wait()


def item_core_kernel(own_ref, code_ref, own_out, p1, p2, p3):
    part = own_out.shape[0]
    for k, out in enumerate((own_out, p1, p2, p3)):
        code = code_ref.at[pl.ds(k * (part + TAIL), part + TAIL)]
        total = own_ref[k * part:(k + 1) * part, :] + decode(code)
        if k == 0:
            out[...] = total
        else:
            encode(out, total)


def item_mid_kernel(own_ref, c1, c2, c3, own_out, p1, p2, p3):
    part = own_out.shape[0]
    total = (own_ref[...] + decode(c1)) + (decode(c2) + decode(c3))
    own_out[...] = total[:part]
    for k, out in enumerate((p1, p2, p3)):
        encode(out, total[(k + 1) * part:(k + 2) * part])


def smem():
    return pl.BlockSpec(memory_space=pltpu.SMEM)


def vmem():
    return pl.BlockSpec(memory_space=pltpu.VMEM)


def anywhere():
    return pl.BlockSpec(memory_space=pl.ANY)


def f32(*shape):
    return jax.ShapeDtypeStruct(shape, jnp.float32)


def i32(*shape):
    return jax.ShapeDtypeStruct(shape, jnp.int32)


def i16(*shape):
    return jax.ShapeDtypeStruct(shape, jnp.int16)


def local(user_factors, item_factors, confidence, tile_counts, tile_user, tile_item, block_slot, live_tiles):
    rows, rank = user_factors.shape
    tiles, edge = confidence.shape[2:4]
    blocks = rows // edge
    pairs = ((tiles + (GROUP - 1) * blocks) // GROUP + UNROLL - 1) // UNROLL * UNROLL + UNROLL
    users_size = lax.axis_size("users")
    items_size = lax.axis_size("items")
    spots = range(users_size)

    def along_y(a, k):
        return lax.ppermute(a, "items", [(i, (i + k) % items_size) for i in range(items_size)])

    def move(i, by_z, k):
        z, x, core = i // 8, i // 2 % 4, i % 2
        if by_z:
            z = (z + k) % 4
        else:
            x = (x + k) % 4
        return z * 8 + x * 2 + core

    def along_first(a, k):
        return lax.ppermute(a, "users", [(i, move(i, i % 2 == 0, k)) for i in spots])

    def along_second(a, k):
        return lax.ppermute(a, "users", [(i, move(i, i % 2 == 1, k)) for i in spots])

    def to_core(a):
        return lax.ppermute(a, "users", [(i, i ^ 1) for i in spots])

    where = lax.broadcasted_iota(jnp.int32, (2,), 0)
    here = jnp.where(where == 0, lax.axis_index("users"), lax.axis_index("items")).astype(jnp.int32)

    own = item_factors[0]
    first = [own] + [along_first(own, k) for k in (1, 2, 3)]
    spot_total = -(-(max(GROUP * pairs, tiles + (GROUP - 1) * users_size) + GROUP * (SLOTS + UNROLL + TURNS)) // 128) * 128
    plan = pl.pallas_call(
        plan_kernel,
        out_shape=(i32(1, 128), i32(1, 128), i32(1, spot_total), i32(1, spot_total), f32(1, spot_total), i32(1, 128), i32(1, spot_total), i32(1, spot_total)),
        in_specs=[smem()] * 2 + [vmem()] * 4,
        out_specs=[vmem()] * 8,
        name="plan",
    )(here, live_tiles[0], tile_user[0], tile_item[0], tile_counts[0], block_slot)
    first = jnp.stack(first)
    first, plan = lax.optimization_barrier((first, plan))
    pieces = [first] + [along_second(first, k) for k in (1, 2, 3)]
    pieces += [to_core(a) for a in pieces]

    quarter = rows // 4
    panels = users_size
    half_rows = panels * edge // 2
    part = half_rows // 4
    user_own, *user_parts, item_own, item_code = pl.pallas_call(
        tile_kernel,
        out_shape=(f32(quarter, rank),)
        + (i16(quarter + TAIL, rank),) * 3
        + (f32(half_rows, rank), i16(4 * (part + TAIL), rank)),
        in_specs=[smem()] * 8 + [vmem(), anywhere()] + [anywhere()] * 8,
        out_specs=[vmem()] * 6,
        scratch_shapes=[
            pltpu.VMEM((panels, edge, rank), jnp.bfloat16),
            pltpu.VMEM((rows, rank), jnp.float32),
            pltpu.VMEM((panels * edge, rank), jnp.float32),
            pltpu.VMEM((SLOTS, GROUP, edge, edge), jnp.bfloat16),
            pltpu.VMEM((GROUP * pairs, edge, edge), jnp.bfloat16),
            pltpu.SemaphoreType.DMA((SLOTS,)),
            pltpu.SemaphoreType.DMA((8,)),
        ],
        name="tiles",
    )(*plan, user_factors, confidence[0, 0], *pieces)

    item_code = to_core(item_code)
    user_parts = [along_y(a, -k) for k, a in zip((1, 2, 3), user_parts)]

    user_code = pl.pallas_call(
        user_sum_kernel,
        out_shape=i16(quarter + TAIL, rank),
        in_specs=[vmem()] * 4,
        out_specs=vmem(),
        name="user_sum",
    )(user_own, *user_parts)

    def item_stage(kernel, size, *ins):
        return pl.pallas_call(
            kernel,
            out_shape=(f32(size, rank),) + (i16(size + TAIL, rank),) * 3,
            in_specs=[vmem()] * len(ins),
            out_specs=[vmem()] * 4,
        )(*ins)

    item_own, *item_parts = item_stage(item_core_kernel, part, item_own, item_code)
    item_parts = [along_second(a, -k) for k, a in zip((1, 2, 3), item_parts)]
    user_codes = [user_code] + [along_y(user_code, k) for k in (1, 2, 3)]
    item_own, *item_parts = item_stage(item_mid_kernel, edge, item_own, *item_parts)
    item_parts = [along_first(a, -k) for k, a in zip((1, 2, 3), item_parts)]
    user_grad, item_grad = pl.pallas_call(
        final_kernel,
        out_shape=(f32(rows, rank), f32(edge, rank)),
        in_specs=[smem()] + [vmem()] * 8,
        out_specs=[anywhere(), vmem()],
        scratch_shapes=[pltpu.VMEM((4, quarter, rank), jnp.float32), pltpu.SemaphoreType.DMA((4,))],
        name="final",
    )(here, *user_codes, item_own, *item_parts)
    return user_grad, item_grad[None]


def solution(mesh):
    in_specs = (
        P("users", None),
        P("items", "users", None),
        P("users", "items", None, None, None),
        P("users", "items", None),
        P("users", "items", None),
        P("users", "items", None),
        P("items", None),
        P("users", "items"),
    )
    out_specs = (P("users", None), P("items", "users", None))

    return jax.shard_map(local, mesh=mesh, in_specs=in_specs, out_specs=out_specs, check_vma=False)
```

```python
import jax
import jax.numpy as jnp
from jax import lax
from jax.experimental import pallas as pl
from jax.experimental.pallas import tpu as pltpu
from jax.sharding import PartitionSpec as P


GRAD_SCALE = 0.005
GRAM_WEIGHT = 0.5
SLOTS = 8
GROUP = 4
UNROLL = 2
TURNS = 16
RING = 4
TAIL = 16
TOP = 32000.0
VMEM_BYTES = 64*1024*1024


def dot(a, b, ca, cb):
    return lax.dot_general(a, b, (((ca,), (cb,)), ((), ())), preferred_element_type=jnp.float32)


def split(x):
    high = x.astype(jnp.bfloat16)
    return high, (x - high.astype(jnp.float32)).astype(jnp.bfloat16)


def encode(out_ref, x):
    rows = x.shape[0]
    top = jnp.max(jnp.abs(x), axis=0, keepdims=True)
    power = jnp.ceil(jnp.log2(jnp.maximum(top, 1e-30) * (1.0 / TOP)))
    out_ref[:rows, :] = jnp.round(x * jnp.exp2(-power)).astype(jnp.int32).astype(jnp.int16)
    tail = jnp.broadcast_to(power, (TAIL, x.shape[1]))
    out_ref[rows:, :] = tail.astype(jnp.int32).astype(jnp.int16)


def decode(ref):
    rows = ref.shape[0] - TAIL
    power = ref[rows:, :].astype(jnp.int32).astype(jnp.float32)[:1]
    return ref[:rows, :].astype(jnp.int32).astype(jnp.float32) * jnp.exp2(power)


def plan_kernel(here_ref, live_ref, user_ref, item_ref, count_ref, slot_ref, head_ref, pair_ref, tile_ref, panel_ref, factor_ref, group_ref, weight_ref, block_ref):
    tiles = user_ref.shape[1]
    spots = tile_ref.shape[1]
    panels = slot_ref.shape[1]
    z = here_ref[0] // 8
    x = (here_ref[0] // 2) & 3
    core = here_ref[0] & 1

    def grid(rows, lanes, axis):
        return lax.broadcasted_iota(jnp.int32, (rows, lanes), axis)

    down = grid(tiles, tiles, 0)
    across = grid(tiles, tiles, 1)

    def pick(mask, values, axis):
        return jnp.sum(jnp.where(mask, values, 0.0), axis=axis, keepdims=True)

    def column(row):
        return pick(down == across, row.astype(jnp.float32), 1)

    user_row = user_ref[...]
    user = column(user_row)
    user_int = user.astype(jnp.int32)
    order = grid(tiles, 1, 0)
    used = order < live_ref[0]
    rank = pick((user_int == user_row) & (across < down), jnp.ones((1, 1), jnp.float32), 1)
    own = (user_int == grid(tiles, 128, 1)) & used
    sizes = pick(own, jnp.ones((1, 1), jnp.float32), 0).astype(jnp.int32)
    groups = ((sizes + (GROUP - 1)) // GROUP).astype(jnp.float32)
    first = pick(grid(tiles, 128, 1) < user_int, groups, 1)
    spot = jnp.where(used, GROUP * first + rank, -1.0).astype(jnp.int32)
    item = column(item_ref[...]).astype(jnp.int32)
    slot = pick(item == grid(tiles, panels, 1), slot_ref[...].astype(jnp.float32), 1).astype(jnp.int32)
    far_z = (z - (slot >> 3)) & 3
    far_x = (x - (slot >> 1)) & 3
    odd = (slot & 1) == 1
    panel = ((core + slot) & 1) * 16 + jnp.where(odd, far_z * 4 + far_x, far_x * 4 + far_z)
    factor = jnp.log(1.0 + column(count_ref[...]))
    at = spot == grid(tiles, spots, 1)
    tile_ref[...] = pick(at, order.astype(jnp.float32), 0).astype(jnp.int32)
    panel_ref[...] = pick(at, panel.astype(jnp.float32), 0).astype(jnp.int32)
    factor_ref[...] = pick(at, factor, 0)
    pair_ref[...] = pick(spot == GROUP * grid(tiles, pair_ref.shape[1], 1), user, 0).astype(jnp.int32)
    total = jnp.sum(groups, axis=1, keepdims=True)
    empty = GROUP * total
    panel_row = pick(down == across, panel.astype(jnp.float32), 0).astype(jnp.int32)
    rank = pick((panel == panel_row) & (across < down), jnp.ones((1, 1), jnp.float32), 1)
    own = (panel == grid(tiles, 128, 1)) & used
    sizes = pick(own, jnp.ones((1, 1), jnp.float32), 0).astype(jnp.int32)
    groups = ((sizes + (GROUP - 1)) // GROUP).astype(jnp.float32)
    first = pick(grid(tiles, 128, 1) < panel, groups, 1)
    place = jnp.where(used, GROUP * first + rank, -1.0).astype(jnp.int32)
    at = place == grid(tiles, spots, 1)
    weight_ref[...] = (pick(at, spot.astype(jnp.float32) - empty, 0) + empty).astype(jnp.int32)
    block_ref[...] = pick(at, user, 0).astype(jnp.int32)
    group_ref[...] = pick(place == GROUP * grid(tiles, 128, 1), panel.astype(jnp.float32), 0).astype(jnp.int32)
    lane = grid(1, 128, 1)
    item_total = jnp.sum(groups, axis=1, keepdims=True)
    numbers = jnp.where(lane == 0, total, item_total).astype(jnp.int32)
    users_rounded = (numbers + (UNROLL - 1)) // UNROLL * UNROLL
    items_rounded = (numbers + (TURNS - 1)) // TURNS * TURNS
    head_ref[...] = jnp.where(lane == 1, here_ref[1], jnp.where(lane == 0, users_rounded, items_rounded))


def loads_of(piece_refs, items_ref, sems):
    return [
        pltpu.make_async_copy(piece, items_ref.at[pl.ds(RING * i, RING)], sems.at[i])
        for i, piece in enumerate(piece_refs)
    ]


def user_gram_kernel(users_ref, out_ref):
    rank = users_ref.shape[1]
    gram = dot(users_ref[...], users_ref[...], 0, 0)
    out_ref[:rank, :], out_ref[rank:, :] = split(GRAM_WEIGHT * gram)


def tile_kernel(*refs):
    head_ref, pair_ref, tile_ref, panel_ref, factor_ref, group_ref, spot_ref, block_ref, users_hbm, conf_ref, gram_ref = refs[:11]
    piece_refs = refs[11:19]
    user_outs = refs[19:23]
    item_own, item_code = refs[23:25]
    users_ref, items_ref, user_acc, item_acc, conf_buf, weights_ref, user_codes, item_codes = refs[25:33]
    sems, piece_sems, out_sems = refs[33:]
    users_load = pltpu.make_async_copy(users_hbm, users_ref, piece_sems.at[8])
    users_load.start()
    edge = conf_buf.shape[2]
    rank = users_ref.shape[1]
    groups = head_ref[0, 0]
    y = head_ref[0, 1]

    loads = loads_of(piece_refs, items_ref, piece_sems)
    for c in loads:
        c.start()

    def fetch(p):
        slot = lax.rem(p, SLOTS)
        for k in range(GROUP):
            tile = tile_ref[0, GROUP * p + k]
            pltpu.make_async_copy(conf_ref.at[tile], conf_buf.at[slot, k], sems.at[slot]).start()

    def arrive(p):
        slot = lax.rem(p, SLOTS)
        pltpu.make_async_copy(conf_ref.at[pl.ds(0, GROUP)], conf_buf.at[slot], sems.at[slot]).wait()

    for s in range(SLOTS):
        fetch(s)

    item_acc[...] = jnp.zeros(item_acc.shape, jnp.float32)
    users_load.wait()
    item_gram = jnp.zeros((rank, rank), jnp.float32)
    for i, c in enumerate(loads):
        c.wait()
        rows = items_ref[RING * i:RING * (i + 1)].reshape(-1, rank)
        item_gram = item_gram + dot(rows, rows, 0, 0)
    high, low = split(GRAM_WEIGHT * item_gram)
    quarter = user_acc.shape[0] // RING
    for k in range(RING):
        q = pl.multiple_of(((y - k) & 3) * quarter, quarter)
        rows = users_ref[pl.ds(q, quarter), :]
        user_acc[k * quarter:(k + 1) * quarter, :] = dot(rows, high, 1, 0) + dot(rows, low, 1, 0)

    def prepare(g):
        slot = lax.rem(g, SLOTS)
        u = pl.multiple_of(pair_ref[0, g] * edge, edge)
        users = users_ref[pl.ds(u, edge), :]
        scores = []
        for j in range(GROUP // 2):
            v0 = panel_ref[0, GROUP * g + 2 * j]
            v1 = panel_ref[0, GROUP * g + 2 * j + 1]
            items = jnp.concatenate([items_ref[v0], items_ref[v1]], axis=0)
            scores.append(dot(users, items, 1, 1))
        for k in range(GROUP):
            part = scores[k // 2][:, (k % 2) * edge:(k % 2 + 1) * edge]
            weight = conf_buf[slot, k].astype(jnp.float32) * factor_ref[0, GROUP * g + k] * (part - 1.0)
            weights_ref[GROUP * g + k] = weight.astype(jnp.bfloat16)

    for j in range(UNROLL):
        arrive(j)
    for j in range(UNROLL):
        prepare(j)

    def visit(i, carry):
        base = i * UNROLL
        for j in range(UNROLL):
            arrive(base + UNROLL + j)
        for j in range(UNROLL):
            fetch(base + j + SLOTS)
        terms = []
        for j in range(UNROLL):
            g = base + j
            items = jnp.concatenate([items_ref[panel_ref[0, GROUP * g + k]] for k in range(GROUP)], axis=0)
            weights = jnp.concatenate([weights_ref[GROUP * g + k] for k in range(GROUP)], axis=1)
            terms.append(dot(weights, items, 1, 0))
        for j in range(UNROLL):
            prepare(base + UNROLL + j)
        for j in range(UNROLL):
            b = pair_ref[0, base + j]
            r = pl.multiple_of(((((y - (b >> 2)) & 3) << 2) + (b & 3)) * edge, edge)
            user_acc[pl.ds(r, edge), :] += terms[j]
        return carry

    lax.fori_loop(0, groups // UNROLL, visit, 0)
    for j in range(UNROLL, SLOTS):
        arrive(groups + j)

    sends = [pltpu.make_async_copy(user_acc.at[pl.ds(0, quarter)], user_outs[0], out_sems.at[0])]
    sends[0].start()
    for k in range(1, RING):
        encode(user_codes.at[k - 1], user_acc[k * quarter:(k + 1) * quarter, :])
        sends.append(pltpu.make_async_copy(user_codes.at[k - 1], user_outs[k], out_sems.at[k]))
        sends[-1].start()

    def turn(i, carry):
        base = i * TURNS
        terms = []
        for j in range(TURNS):
            g = base + j
            parts = []
            for k in range(GROUP):
                u = pl.multiple_of(block_ref[0, GROUP * g + k] * edge, edge)
                parts.append(users_ref[pl.ds(u, edge), :])
            weights = jnp.concatenate([weights_ref[spot_ref[0, GROUP * g + k]] for k in range(GROUP)], axis=0)
            terms.append(dot(weights, jnp.concatenate(parts, axis=0), 0, 0))
        for j in range(TURNS):
            r = pl.multiple_of(group_ref[0, base + j] * edge, edge)
            item_acc[pl.ds(r, edge), :] += terms[j]
        return carry

    lax.fori_loop(0, head_ref[0, 2] // TURNS, turn, 0)
    user_high = gram_ref[:rank, :]
    user_low = gram_ref[rank:, :]
    part = item_acc.shape[0] // 8
    for k in range(8):
        items = items_ref[RING * k:RING * (k + 1)].reshape(part, rank)
        total = item_acc[k * part:(k + 1) * part, :] + (dot(items, user_high, 1, 0) + dot(items, user_low, 1, 0))
        if k < RING:
            rows = pl.ds(k * part, part)
            item_acc[k * part:(k + 1) * part, :] = total
            send = pltpu.make_async_copy(item_acc.at[rows], item_own.at[rows], out_sems.at[RING + k])
        else:
            rows = pl.ds((k - RING) * (part + TAIL), part + TAIL)
            encode(item_codes.at[rows], total)
            send = pltpu.make_async_copy(item_codes.at[rows], item_code.at[rows], out_sems.at[RING + k])
        send.start()
        sends.append(send)
    for send in sends:
        send.wait()


def user_sum_kernel(own_ref, p1, p2, p3, out_ref):
    encode(out_ref, (own_ref[...] + decode(p1)) + (decode(p2) + decode(p3)))


def final_kernel(here_ref, p0, p1, p2, p3, own_ref, q1, q2, q3, user_out, item_out, buf, sems):
    quarter = p0.shape[0] - TAIL
    copies = []
    for k, p in enumerate((p0, p1, p2, p3)):
        buf[k] = GRAD_SCALE * decode(p)
        q = pl.multiple_of(((here_ref[1] - k) & 3) * quarter, quarter)
        copies.append(pltpu.make_async_copy(buf.at[k], user_out.at[pl.ds(q, quarter)], sems.at[k]))
        copies[-1].start()
    item_out[...] = GRAD_SCALE * ((own_ref[...] + decode(q1)) + (decode(q2) + decode(q3)))
    for c in copies:
        c.wait()


def item_core_kernel(own_ref, code_ref, own_out, p1, p2, p3, own_buf, code_buf, codes, in_sems, out_sems):
    part = own_out.shape[0]
    order = (1, 2, 3, 0)
    loads = {}
    for k in order:
        rows = pl.ds(k * part, part)
        coded = pl.ds(k * (part + TAIL), part + TAIL)
        loads[k] = (
            pltpu.make_async_copy(own_ref.at[rows], own_buf.at[k], in_sems.at[k]),
            pltpu.make_async_copy(code_ref.at[coded], code_buf.at[k], in_sems.at[4 + k]),
        )
        for c in loads[k]:
            c.start()
    sends = []
    for k in order:
        for c in loads[k]:
            c.wait()
        total = own_buf[k] + decode(code_buf.at[k])
        if k == 0:
            own_buf[k] = total
            sends.append(pltpu.make_async_copy(own_buf.at[k], own_out, out_sems.at[k]))
        else:
            encode(codes.at[k - 1], total)
            sends.append(pltpu.make_async_copy(codes.at[k - 1], (p1, p2, p3)[k - 1], out_sems.at[k]))
        sends[-1].start()
    for c in sends:
        c.wait()


def item_mid_kernel(own_ref, c1, c2, c3, own_out, p1, p2, p3):
    part = own_out.shape[0]
    total = (own_ref[...] + decode(c1)) + (decode(c2) + decode(c3))
    own_out[...] = total[:part]
    for k, out in enumerate((p1, p2, p3)):
        encode(out, total[(k + 1) * part:(k + 2) * part])


def smem():
    return pl.BlockSpec(memory_space=pltpu.SMEM)


def vmem():
    return pl.BlockSpec(memory_space=pltpu.VMEM)


def anywhere():
    return pl.BlockSpec(memory_space=pl.ANY)


def f32(*shape):
    return jax.ShapeDtypeStruct(shape, jnp.float32)


def i32(*shape):
    return jax.ShapeDtypeStruct(shape, jnp.int32)


def i16(*shape):
    return jax.ShapeDtypeStruct(shape, jnp.int16)


def local(user_factors, item_factors, confidence, tile_counts, tile_user, tile_item, block_slot, live_tiles):
    rows, rank = user_factors.shape
    tiles, edge = confidence.shape[2:4]
    blocks = rows // edge
    pairs = ((tiles + (GROUP - 1) * blocks) // GROUP + UNROLL - 1) // UNROLL * UNROLL + UNROLL
    users_size = lax.axis_size("users")
    items_size = lax.axis_size("items")
    spots = range(users_size)

    def along_y(a, k):
        return lax.ppermute(a, "items", [(i, (i + k) % items_size) for i in range(items_size)])

    def move(i, by_z, k):
        z, x, core = i // 8, i // 2 % 4, i % 2
        if by_z:
            z = (z + k) % 4
        else:
            x = (x + k) % 4
        return z * 8 + x * 2 + core

    def along_first(a, k):
        return lax.ppermute(a, "users", [(i, move(i, i % 2 == 0, k)) for i in spots])

    def along_second(a, k):
        return lax.ppermute(a, "users", [(i, move(i, i % 2 == 1, k)) for i in spots])

    def to_core(a):
        return lax.ppermute(a, "users", [(i, i ^ 1) for i in spots])

    where = lax.broadcasted_iota(jnp.int32, (2,), 0)
    here = jnp.where(where == 0, lax.axis_index("users"), lax.axis_index("items")).astype(jnp.int32)

    own = item_factors[0]
    first = [own] + [along_first(own, k) for k in (1, 2, 3)]
    spot_total = -(-(max(GROUP * pairs, tiles + (GROUP - 1) * users_size) + GROUP * (SLOTS + UNROLL + TURNS)) // 128) * 128
    plan = pl.pallas_call(
        plan_kernel,
        out_shape=(i32(1, 128), i32(1, 128), i32(1, spot_total), i32(1, spot_total), f32(1, spot_total), i32(1, 128), i32(1, spot_total), i32(1, spot_total)),
        in_specs=[smem()] * 2 + [vmem()] * 4,
        out_specs=[vmem()] * 8,
        name="plan",
    )(here, live_tiles[0], tile_user[0], tile_item[0], tile_counts[0], block_slot)
    first = jnp.stack(first)
    first, plan = lax.optimization_barrier((first, plan))
    user_gram = pl.pallas_call(
        user_gram_kernel,
        out_shape=jax.ShapeDtypeStruct((2 * rank, rank), jnp.bfloat16),
        in_specs=[vmem()],
        out_specs=vmem(),
        name="gram",
        compiler_params=pltpu.CompilerParams(vmem_limit_bytes=VMEM_BYTES),
    )(user_factors)
    pieces = [first] + [along_second(first, k) for k in (1, 2, 3)]
    pieces += [to_core(a) for a in pieces]

    quarter = rows // 4
    panels = users_size
    half_rows = panels * edge // 2
    part = half_rows // 4
    user_own, *user_parts, item_own, item_code = pl.pallas_call(
        tile_kernel,
        out_shape=(f32(quarter, rank),)
        + (i16(quarter + TAIL, rank),) * 3
        + (f32(half_rows, rank), i16(4 * (part + TAIL), rank)),
        in_specs=[smem()] * 8 + [anywhere()] * 2 + [vmem()] + [anywhere()] * 8,
        out_specs=[anywhere()] * 6,
        scratch_shapes=[
            pltpu.VMEM((rows, rank), jnp.bfloat16),
            pltpu.VMEM((panels, edge, rank), jnp.bfloat16),
            pltpu.VMEM((rows, rank), jnp.float32),
            pltpu.VMEM((panels * edge, rank), jnp.float32),
            pltpu.VMEM((SLOTS, GROUP, edge, edge), jnp.bfloat16),
            pltpu.VMEM((GROUP * pairs, edge, edge), jnp.bfloat16),
            pltpu.VMEM((3, quarter + TAIL, rank), jnp.int16),
            pltpu.VMEM((4 * (part + TAIL), rank), jnp.int16),
            pltpu.SemaphoreType.DMA((SLOTS,)),
            pltpu.SemaphoreType.DMA((9,)),
            pltpu.SemaphoreType.DMA((12,)),
        ],
        name="tiles",
        compiler_params=pltpu.CompilerParams(vmem_limit_bytes=VMEM_BYTES),
    )(*plan, user_factors, confidence[0, 0], user_gram, *pieces)

    item_code = to_core(item_code)
    user_parts = [along_y(a, -k) for k, a in zip((1, 2, 3), user_parts)]

    user_code = pl.pallas_call(
        user_sum_kernel,
        out_shape=i16(quarter + TAIL, rank),
        in_specs=[vmem()] * 4,
        out_specs=vmem(),
        name="user_sum",
        compiler_params=pltpu.CompilerParams(vmem_limit_bytes=VMEM_BYTES),
    )(user_own, *user_parts)

    def item_stage(kernel, size, *ins):
        return pl.pallas_call(
            kernel,
            out_shape=(f32(size, rank),) + (i16(size + TAIL, rank),) * 3,
            in_specs=[vmem()] * len(ins),
            out_specs=[vmem()] * 4,
            compiler_params=pltpu.CompilerParams(vmem_limit_bytes=VMEM_BYTES),
        )(*ins)

    item_own, *item_parts = pl.pallas_call(
        item_core_kernel,
        out_shape=(f32(part, rank),) + (i16(part + TAIL, rank),) * 3,
        in_specs=[anywhere()] * 2,
        out_specs=[anywhere()] * 4,
        scratch_shapes=[
            pltpu.VMEM((4, part, rank), jnp.float32),
            pltpu.VMEM((4, part + TAIL, rank), jnp.int16),
            pltpu.VMEM((3, part + TAIL, rank), jnp.int16),
            pltpu.SemaphoreType.DMA((8,)),
            pltpu.SemaphoreType.DMA((4,)),
        ],
        name="item_core",
        compiler_params=pltpu.CompilerParams(vmem_limit_bytes=VMEM_BYTES),
    )(item_own, item_code)
    item_parts = [along_second(a, -k) for k, a in zip((1, 2, 3), item_parts)]
    user_codes = [user_code] + [along_y(user_code, k) for k in (1, 2, 3)]
    item_own, *item_parts = item_stage(item_mid_kernel, edge, item_own, *item_parts)
    item_parts = [along_first(a, -k) for k, a in zip((1, 2, 3), item_parts)]
    user_grad, item_grad = pl.pallas_call(
        final_kernel,
        out_shape=(f32(rows, rank), f32(edge, rank)),
        in_specs=[smem()] + [vmem()] * 8,
        out_specs=[anywhere(), vmem()],
        scratch_shapes=[pltpu.VMEM((4, quarter, rank), jnp.float32), pltpu.SemaphoreType.DMA((4,))],
        name="final",
        compiler_params=pltpu.CompilerParams(vmem_limit_bytes=VMEM_BYTES),
    )(here, *user_codes, item_own, *item_parts)
    return user_grad, item_grad[None]


def solution(mesh):
    in_specs = (
        P("users", None),
        P("items", "users", None),
        P("users", "items", None, None, None),
        P("users", "items", None),
        P("users", "items", None),
        P("users", "items", None),
        P("items", None),
        P("users", "items"),
    )
    out_specs = (P("users", None), P("items", "users", None))

    return jax.shard_map(local, mesh=mesh, in_specs=in_specs, out_specs=out_specs, check_vma=False)
```
